256 devices in a mesh: rows: 256 (over z, x, y, core).
Axes of the slice: x: 4, y: 4, z: 8, core: 2. Of those that a mesh axis runs over, the one named last changes fastest.
Arguments:
- matrix: float32 [1048576, 128], P('rows')
- flips: int32 [1048576], P('rows'), may hold values from 0 to 1
- picks: int32 [16384], P('rows'), may hold values from 0 to 4095, as said below
Outputs:
- sketch: float32 [16384, 128], P('rows')
- factor: float32 [128, 128], replicated
The draws below stay inside these ranges and needn't reach their ends.
Inputs may be any that keep to these rules, and one draw needn't show every extreme that they name: `picks`: each index lies within its owner's slab; repeated indices may occur.
All inputs are finite; a program needn't handle non-finite values.
Results may differ from the reference program's by a relative error of at most 0.00014.
Values sent between devices are 32-bit elements; how exact they have to be, the bound alone decides.
A program may use at most 64 MiB of HBM per device.

```python
import math
import jax
import jax.numpy as jnp
from jax import lax

COLS = 128
ROWS_DEV = 4096
S_DEV = 64
TOTAL_ROWS = 1048576
SAMPLES = 16384


def draw_matrix(key, part):
    key_main, key_rows, key_cols = jax.random.split(key, 3)
    entries = jax.random.normal(key_main, (TOTAL_ROWS, COLS), jnp.float32)
    low = math.log(0.3)
    high = math.log(3.0)
    row_scale = jnp.exp(jax.random.uniform(key_rows, (TOTAL_ROWS, 1), jnp.float32, low, high))
    col_scale = jnp.exp(jax.random.uniform(key_cols, (1, COLS), jnp.float32, low, high))
    return entries * row_scale * col_scale


def draw_picks(key, part):
    key_main, key_first, key_second = jax.random.split(jax.random.fold_in(key, 7), 3)
    chosen = jax.random.randint(key_main, (SAMPLES,), 0, ROWS_DEV, jnp.int32)
    first = jax.random.randint(key_first, (), 0, SAMPLES, jnp.int32)
    offset = jax.random.randint(key_second, (), 1, SAMPLES, jnp.int32)
    second = (first + offset) % SAMPLES
    chosen = chosen.at[first].set(ROWS_DEV - 1)
    chosen = chosen.at[second].set(0)
    return chosen


def touch_ends(array, stream_key, low, top_value):
    spot = [jax.random.randint(jax.random.fold_in(stream_key, axis), (), 0, length) for axis, length in enumerate(array.shape)]
    main_axis = array.shape.index(max(array.shape))
    beside = spot[:main_axis] + [(spot[main_axis] + 1) % array.shape[main_axis]] + spot[main_axis + 1:]
    return array.at[tuple(spot)].set(low).at[tuple(beside)].set(top_value)


def setup_inputs(seed: int = 0) -> dict:
    splits = jax.random.split(jax.random.key(seed), 4)
    return {
        "matrix": draw_matrix(jax.random.fold_in(splits[3], 71), 0),
        "flips": touch_ends(jax.random.randint(splits[1], (TOTAL_ROWS,), 0, 2), jax.random.fold_in(splits[1], 1), 0, 1).astype(jnp.int32),
        "picks": draw_picks(jax.random.fold_in(splits[3], 71), 0),
    }


def reference(matrix, flips, picks):
    signs = (1 - 2 * flips).astype(jnp.float32)
    values = matrix * signs[:, None]
    count = TOTAL_ROWS.bit_length() - 1
    span = 1
    for level in range(count):
        blocks = values.reshape(TOTAL_ROWS // (2 * span), 2, span, COLS)
        first = blocks[:, 0]
        second = blocks[:, 1]
        values = jnp.stack([first + second, first - second], axis=1).reshape(TOTAL_ROWS, COLS)
        span = span * 2
    scale = 1.0 / math.sqrt(TOTAL_ROWS)
    owners = jnp.arange(SAMPLES, dtype=jnp.int32) // S_DEV
    chosen = owners * ROWS_DEV + picks.astype(jnp.int32)
    sketch = jnp.take(values, chosen, axis=0) * scale
    gram = jnp.dot(sketch.T.astype(jnp.float32), sketch.astype(jnp.float32), preferred_element_type=jnp.float32, precision=lax.Precision.HIGHEST) / SAMPLES
    factor = jnp.linalg.cholesky(gram)
    return (sketch, factor)
```

```python
import jax
import jax.numpy as jnp
from jax import lax
from jax.experimental import pallas as pl
from jax.experimental.pallas import tpu as pltpu
from jax.sharding import PartitionSpec as P

MESH = pl.DeviceIdType.MESH
F32 = jnp.float32
BF16 = jnp.bfloat16

RING = 4
DEPTH = 8
ROWS = 4096
COLS = 128
PER = 64
BLOCK = 256
BLOCKS = ROWS // BLOCK
CHUNKS = 8
CHUNK = ROWS // CHUNKS
PART_A = RING * DEPTH * PER // 2
PART_B = DEPTH * PER // 2
PIECE = COLS // RING


def parity_sign(left, right):
    both = left & right
    both = (both ^ (both >> 1) ^ (both >> 2)) & 1
    return (1 - 2 * both).astype(F32)


def hadamard_block():
    row = lax.broadcasted_iota(jnp.int32, (BLOCK, BLOCK), 0)
    col = lax.broadcasted_iota(jnp.int32, (BLOCK, BLOCK), 1)
    both = row & col
    both = both ^ (both >> 4)
    both = both ^ (both >> 2)
    both = both ^ (both >> 1)
    return (1 - 2 * (both & 1)).astype(F32).astype(BF16)


def kernel(
    mat, flips, picks, sketch, gram,
    own, par, flips_par, had, mixed, picked, picked_s,
    out_a, opp_a, from_left_a, from_right_a, tot_a,
    out_b, opp_b, from_left_b, from_right_b, tot_b,
    got_z, part_g, got_ga, piece_b, piece_z, full_g, other_g,
    load_sem, core_send, core_recv, flip_sems, pick_send, pick_recv, pick_local,
    a_send, a_recv, b_send, b_recv, z_send, z_recv, g_send, g_recv,
):
    me = lax.axis_index("rows")
    core = lax.rem(me, 2)
    ypos = lax.rem(lax.div(me, 2), RING)
    xpos = lax.rem(lax.div(me, 2 * RING), RING)
    z = lax.div(me, 2 * RING * RING)
    a = ypos + core * (xpos - ypos)
    b = xpos + core * (ypos - xpos)
    step_a = 2 + core * (2 * RING - 2)
    step_b = 2 * RING - core * (2 * RING - 2)
    partner = me + 1 - 2 * core

    def turn(position, by, size):
        return lax.rem(position + by, size)

    def peer_a(by):
        return me + (turn(a, by, RING) - a) * step_a

    def peer_b(by):
        return me + (turn(b, by, RING) - b) * step_b

    def peer_z(by):
        return me + (turn(z, by, DEPTH) - z) * (2 * RING * RING)

    def remote(src, dst, send, recv, device):
        return pltpu.make_async_remote_copy(
            src_ref=src, dst_ref=dst, send_sem=send, recv_sem=recv,
            device_id=(device,), device_id_type=MESH,
        )

    loads = []
    for k in range(CHUNKS):
        rows = pl.ds(k * CHUNK, CHUNK)
        load = pltpu.make_async_copy(mat.at[rows], own.at[rows], load_sem.at[k])
        load.start()
        loads.append(load)

    barrier = pltpu.get_barrier_semaphore()
    peers = [partner] + [peer_a(k) for k in range(1, RING)] + [peer_b(k) for k in range(1, RING)]
    peers += [peer_z(k) for k in range(1, DEPTH)]
    for device in peers:
        pl.semaphore_signal(barrier, inc=1, device_id=(device,), device_id_type=MESH)

    had[...] = hadamard_block()

    def transformed(block, values, flip_ref, sign):
        negative = jnp.concatenate([flip_ref[pl.ds(2 * block, 1), :], flip_ref[pl.ds(2 * block + 1, 1), :]], axis=1)
        signs = ((1 - 2 * negative).astype(F32) * sign).astype(BF16)
        high = values.astype(BF16)
        low = (values - high.astype(F32)).astype(BF16)
        both = jnp.concatenate([high, low], axis=1)
        product = jnp.dot(had[...] * signs, both, preferred_element_type=F32)
        return product[:, :COLS] + product[:, COLS:]

    own_sign = parity_sign(core, core)
    par_sign = jnp.float32(1.0)
    for k in range(CHUNKS):
        loads[k].wait()
        for j in range(CHUNK // BLOCK):
            block = k * (CHUNK // BLOCK) + j
            rows = pl.ds(block * BLOCK, BLOCK)
            mixed[rows, :] = transformed(block, own[rows, :], flips, own_sign)

    pl.semaphore_wait(barrier, len(peers))

    flip_copy = remote(flips, flips_par, flip_sems.at[0], flip_sems.at[1], partner)
    flip_copy.start()
    core_copies = []
    for k in range(CHUNKS):
        rows = pl.ds(k * CHUNK, CHUNK)
        copy = remote(mat.at[rows], par.at[rows], core_send.at[k], core_recv.at[k], partner)
        copy.start()
        core_copies.append(copy)

    slot = (z * RING + b) * RING + a
    keep = pltpu.make_async_copy(picks, picked.at[slot], pick_local.at[0])
    keep.start()
    picks_a = []
    for k in range(1, RING):
        copy = remote(picks, picked.at[slot], pick_send.at[k - 1], pick_recv.at[k - 1], peer_a(k))
        copy.start()
        picks_a.append(copy)

    def fold(k):
        for j in range(CHUNK // BLOCK):
            block = k * (CHUNK // BLOCK) + j
            rows = pl.ds(block * BLOCK, BLOCK)
            mixed[rows, :] += transformed(block, par[rows, :], flips_par, par_sign)

    flip_copy.wait()
    keep.wait()
    for k in range(2):
        core_copies[k].wait()
        fold(k)
    for copy in picks_a:
        copy.wait()
    picks_b = []
    line = pl.ds((z * RING + b) * RING, RING)
    for k in range(1, RING):
        copy = remote(picked.at[line], picked.at[line], pick_send.at[k + 2], pick_recv.at[k + 2], peer_b(k))
        copy.start()
        picks_b.append(copy)
    for k in range(2, 5):
        core_copies[k].wait()
        fold(k)
    for copy in picks_b:
        copy.wait()
    picks_z = []
    plane = pl.ds(z * RING * RING, RING * RING)
    for k in range(1, DEPTH):
        copy = remote(picked.at[plane], picked.at[plane], pick_send.at[k + 5], pick_recv.at[k + 5], peer_z(k))
        copy.start()
        picks_z.append(copy)
    for k in range(5, CHUNKS):
        core_copies[k].wait()
        fold(k)

    def butterfly(i, carry):
        values = [mixed[pl.ds(j * BLOCK + pl.multiple_of(i * 8, 8), 8), :] for j in range(BLOCKS)]
        span = 1
        while span < BLOCKS:
            after = list(values)
            for j in range(BLOCKS):
                if not j & span:
                    after[j] = values[j] + values[j + span]
                    after[j + span] = values[j] - values[j + span]
            values = after
            span *= 2
        for j in range(BLOCKS):
            mixed[pl.ds(j * BLOCK + pl.multiple_of(i * 8, 8), 8), :] = values[j]
        return carry

    lax.fori_loop(0, BLOCK // 8, butterfly, 0)

    for copy in picks_z:
        copy.wait()
    to_scalar = pltpu.make_async_copy(picked, picked_s, pick_local.at[1])
    to_scalar.start()
    to_scalar.wait()

    def gather(dst, base, dest, half):
        sign = parity_sign(dest, a)

        def body(q, carry):
            b_to = half * (RING // 2) + lax.div(q, DEPTH)
            z_to = lax.rem(q, DEPTH)
            place = (z_to * RING + b_to) * RING + dest
            for g in range(PER // 16):
                rows = [mixed[pl.ds(picked_s[place, 0, g * 16 + s], 1), :] for s in range(16)]
                for s in range(16):
                    dst[pl.ds(base + q * PER + g * 16 + s, 1), :] = rows[s] * sign
            return carry

        lax.fori_loop(0, RING // 2 * DEPTH, body, 0)

    right, left = peer_a(1), peer_a(RING - 1)
    at_right, at_left, at_opp = turn(a, 1, RING), turn(a, 3, RING), turn(a, 2, RING)

    def send_a(k, dst, device):
        copy = remote(out_a.at[k], dst, a_send.at[k], a_recv.at[k], device)
        copy.start()
        return copy

    gather(out_a.at[0], 0, at_opp, 0)
    c0 = send_a(0, opp_a.at[0], right)
    gather(out_a.at[1], 0, at_opp, 1)
    c1 = send_a(1, opp_a.at[1], left)
    gather(out_a.at[2], 0, at_right, 1)
    c2 = send_a(2, from_left_a.at[1], right)
    gather(out_a.at[3], 0, at_left, 0)
    c3 = send_a(3, from_right_a.at[0], left)
    gather(out_a.at[4], 0, at_right, 0)
    c0.wait_recv()
    out_a[4] += opp_a[0]
    c4 = send_a(4, from_left_a.at[0], right)
    gather(out_a.at[5], 0, at_left, 1)
    c1.wait_recv()
    out_a[5] += opp_a[1]
    c5 = send_a(5, from_right_a.at[1], left)
    gather(tot_a, 0, a, 0)
    gather(tot_a, PART_A, a, 1)
    c2.wait_recv()
    c3.wait_recv()

    def total_a(half):
        for j in range(RING // 2):
            b_to = half * (RING // 2) + j
            rows = pl.ds(b_to * 2 * PART_B, 2 * PART_B)
            inner = pl.ds(j * 2 * PART_B, 2 * PART_B)
            summed = tot_a[rows, :] + from_left_a[half, inner, :] + from_right_a[half, inner, :]
            tot_a[rows, :] = summed * parity_sign(jnp.int32(b_to), b)

    c4.wait_recv()
    total_a(0)
    c5.wait_recv()
    total_a(1)

    b_right, b_left, b_opp = turn(b, 1, RING), turn(b, 3, RING), turn(b, 2, RING)
    right_b, left_b = peer_b(1), peer_b(RING - 1)

    def rows_b(dest, half):
        return pl.ds(pl.multiple_of(dest * (2 * PART_B) + half * PART_B, 8), PART_B)

    def send_b(k, src, dst, device):
        copy = remote(src, dst, b_send.at[k], b_recv.at[k], device)
        copy.start()
        return copy

    d0 = send_b(0, tot_a.at[rows_b(b_opp, 0)], opp_b.at[0], right_b)
    d1 = send_b(1, tot_a.at[rows_b(b_opp, 1)], opp_b.at[1], left_b)
    d2 = send_b(2, tot_a.at[rows_b(b_right, 1)], from_left_b.at[1], right_b)
    d3 = send_b(3, tot_a.at[rows_b(b_left, 0)], from_right_b.at[0], left_b)
    d0.wait_recv()
    out_b[0] = tot_a[rows_b(b_right, 0), :] + opp_b[0]
    d4 = send_b(4, out_b.at[0], from_left_b.at[0], right_b)
    d1.wait_recv()
    out_b[1] = tot_a[rows_b(b_left, 1), :] + opp_b[1]
    d5 = send_b(5, out_b.at[1], from_right_b.at[1], left_b)
    d2.wait_recv()
    d3.wait_recv()

    def total_b(half):
        for j in range(DEPTH // 2):
            z_to = half * (DEPTH // 2) + j
            inner = pl.ds(j * PER, PER)
            own_rows = pl.ds(pl.multiple_of(b * (2 * PART_B) + z_to * PER, 8), PER)
            summed = tot_a[own_rows, :] + from_left_b[half, inner, :] + from_right_b[half, inner, :]
            tot_b[z_to] = summed * parity_sign(jnp.int32(z_to), z)

    d4.wait_recv()
    total_b(0)
    d5.wait_recv()
    total_b(1)

    z_copies = []
    for k in (4, 3, 5, 2, 6, 1, 7):
        copy = remote(tot_b.at[turn(z, k, DEPTH)], got_z.at[k - 1], z_send.at[k - 1], z_recv.at[k - 1], peer_z(k))
        copy.start()
        z_copies.append(copy)
    for copy in z_copies:
        copy.wait_recv()
    rows = tot_b[z]
    for k in range(DEPTH - 1):
        rows = rows + got_z[k]
    rows = rows * (1.0 / 1024.0)
    sketch[...] = rows

    part_g[...] = lax.dot_general(
        rows, rows, (((0,), (0,)), ((), ())), precision=lax.Precision.HIGHEST, preferred_element_type=F32
    )

    def send_g(k, src, dst, device):
        copy = remote(src, dst, g_send.at[k], g_recv.at[k], device)
        copy.start()
        return copy

    def piece(position):
        return pl.ds(pl.multiple_of(position * PIECE, PIECE), PIECE)

    copies = [send_g(k - 1, part_g.at[piece(turn(a, k, RING))], got_ga.at[k - 1], peer_a(k)) for k in range(1, RING)]
    for copy in copies:
        copy.wait_recv()
    piece_b[b] = part_g[piece(a), :] + got_ga[0] + got_ga[1] + got_ga[2]
    pending = copies
    copies = [send_g(k + 2, piece_b.at[b], piece_b.at[b], peer_b(k)) for k in range(1, RING)]
    for copy in copies:
        copy.wait_recv()
    piece_z[z] = piece_b[0] + piece_b[1] + piece_b[2] + piece_b[3]
    pending = pending + copies
    copies = [send_g(k + 5, piece_z.at[z], piece_z.at[z], peer_z(k)) for k in (4, 3, 5, 2, 6, 1, 7)]
    for copy in copies:
        copy.wait_recv()
    total = piece_z[0]
    for k in range(1, DEPTH):
        total = total + piece_z[k]
    full_g[piece(a), :] = total
    pending = pending + copies
    copies = [send_g(k + 12, full_g.at[piece(a)], full_g.at[piece(a)], peer_a(k)) for k in range(1, RING)]
    for copy in copies:
        copy.wait_recv()
    pending = pending + copies
    last = send_g(16, full_g, other_g, partner)
    last.wait_recv()
    gram[...] = (full_g[...] + other_g[...]) * (1.0 / (PER * 2 * RING * RING * DEPTH))
    pending = pending + [last]

    for copy in [c0, c1, c2, c3, c4, c5, d0, d1, d2, d3, d4, d5] + z_copies + pending:
        copy.wait_send()


def shards(matrix, flips, picks):
    vmem = pl.BlockSpec(memory_space=pltpu.VMEM)
    half_a = (PART_A, COLS)
    half_b = (PART_B, COLS)
    dma = pltpu.SemaphoreType.DMA
    sketch, gram = pl.pallas_call(
        kernel,
        name="blendenpik",
        out_shape=(
            jax.ShapeDtypeStruct((PER, COLS), F32),
            jax.ShapeDtypeStruct((COLS, COLS), F32),
        ),
        in_specs=[pl.BlockSpec(memory_space=pl.ANY), vmem, vmem],
        out_specs=(vmem, vmem),
        scratch_shapes=[
            pltpu.VMEM((ROWS, COLS), F32),
            pltpu.VMEM((ROWS, COLS), F32),
            pltpu.VMEM((ROWS // COLS, COLS), jnp.int32),
            pltpu.VMEM((BLOCK, BLOCK), BF16),
            pltpu.VMEM((ROWS, COLS), F32),
            pltpu.VMEM((RING * RING * DEPTH, 1, PER), jnp.int32),
            pltpu.SMEM((RING * RING * DEPTH, 1, PER), jnp.int32),
            pltpu.VMEM((6, *half_a), F32),
            pltpu.VMEM((2, *half_a), F32),
            pltpu.VMEM((2, *half_a), F32),
            pltpu.VMEM((2, *half_a), F32),
            pltpu.VMEM((2 * PART_A, COLS), F32),
            pltpu.VMEM((2, *half_b), F32),
            pltpu.VMEM((2, *half_b), F32),
            pltpu.VMEM((2, *half_b), F32),
            pltpu.VMEM((2, *half_b), F32),
            pltpu.VMEM((DEPTH, PER, COLS), F32),
            pltpu.VMEM((DEPTH - 1, PER, COLS), F32),
            pltpu.VMEM((COLS, COLS), F32),
            pltpu.VMEM((RING - 1, PIECE, COLS), F32),
            pltpu.VMEM((RING, PIECE, COLS), F32),
            pltpu.VMEM((DEPTH, PIECE, COLS), F32),
            pltpu.VMEM((COLS, COLS), F32),
            pltpu.VMEM((COLS, COLS), F32),
            dma((CHUNKS,)),
            dma((CHUNKS,)),
            dma((CHUNKS,)),
            dma((2,)),
            dma((13,)),
            dma((13,)),
            dma((2,)),
            dma((6,)),
            dma((6,)),
            dma((6,)),
            dma((6,)),
            dma((7,)),
            dma((7,)),
            dma((17,)),
            dma((17,)),
        ],
        compiler_params=pltpu.CompilerParams(
            collective_id=0, has_side_effects=True, vmem_limit_bytes=48 * 1024 * 1024
        ),
    )(matrix, flips.reshape(ROWS // COLS, COLS), picks.reshape(1, PER))
    factor = lax.linalg.cholesky(gram, symmetrize_input=False)
    return (sketch, factor)


def solution(mesh):
    placed = (P("rows", None), P("rows"), P("rows"))
    return jax.shard_map(
        shards, mesh=mesh, in_specs=placed, out_specs=(P("rows", None), P()), check_vma=False
    )
```

```python
import jax
import jax.numpy as jnp
from jax import lax
from jax.experimental import pallas as pl
from jax.experimental.pallas import tpu as pltpu
from jax.sharding import PartitionSpec as P

MESH = pl.DeviceIdType.MESH
F32 = jnp.float32
BF16 = jnp.bfloat16

RING = 4
DEPTH = 8
ROWS = 4096
COLS = 128
PER = 64
BLOCK = 256
BLOCKS = ROWS // BLOCK
CHUNKS = 8
CHUNK = ROWS // CHUNKS
PART_A = RING * DEPTH * PER // 2
PART_B = DEPTH * PER // 2
PIECE = COLS // RING
PANEL = 16


def parity_sign(left, right):
    both = left & right
    both = (both ^ (both >> 1) ^ (both >> 2)) & 1
    return (1 - 2 * both).astype(F32)


def hadamard_block():
    row = lax.broadcasted_iota(jnp.int32, (BLOCK, BLOCK), 0)
    col = lax.broadcasted_iota(jnp.int32, (BLOCK, BLOCK), 1)
    both = row & col
    both = both ^ (both >> 4)
    both = both ^ (both >> 2)
    both = both ^ (both >> 1)
    return (1 - 2 * (both & 1)).astype(F32).astype(BF16)


def kernel(
    mat, flips_in, picks, sketch, gram,
    own, par, flips, flips_par, had, mixed, picked, picked_s,
    out_a, opp_a, from_left_a, from_right_a, tot_a,
    out_b, opp_b, from_left_b, from_right_b, tot_b,
    got_z, part_g, got_ga, piece_b, piece_z, full_g, other_g,
    load_sem, flip_load, go, ready, core_send, core_recv, flip_sems, pick_send, pick_recv, pick_local, scalar_sem,
    a_send, a_recv, b_send, b_recv, z_send, z_recv, g_send, g_recv,
):
    me = lax.axis_index("rows")
    core = lax.rem(me, 2)
    ypos = lax.rem(lax.div(me, 2), RING)
    xpos = lax.rem(lax.div(me, 2 * RING), RING)
    z = lax.div(me, 2 * RING * RING)
    a = ypos + core * (xpos - ypos)
    b = xpos + core * (ypos - xpos)
    step_a = 2 + core * (2 * RING - 2)
    step_b = 2 * RING - core * (2 * RING - 2)
    partner = me + 1 - 2 * core

    def turn(position, by, size):
        return lax.rem(position + by, size)

    def peer_a(by):
        return me + (turn(a, by, RING) - a) * step_a

    def peer_b(by):
        return me + (turn(b, by, RING) - b) * step_b

    def peer_z(by):
        return me + (turn(z, by, DEPTH) - z) * (2 * RING * RING)

    def remote(src, dst, send, recv, device):
        return pltpu.make_async_remote_copy(
            src_ref=src, dst_ref=dst, send_sem=send, recv_sem=recv,
            device_id=(device,), device_id_type=MESH,
        )

    barrier = pltpu.get_barrier_semaphore()
    plane = [peer_a(k) for k in range(1, RING)] + [peer_b(k) for k in range(1, RING)]
    column = [peer_z(k) for k in range(1, DEPTH)]

    def signal(semaphore, device):
        pl.semaphore_signal(semaphore, inc=1, device_id=(device,), device_id_type=MESH)

    @pl.when(core == 0)
    def _():
        for device in plane:
            signal(barrier, device)

    @pl.when(core == 1)
    def _():
        signal(barrier, partner)

    loads = []
    for k in range(CHUNKS):
        rows = pl.ds(k * CHUNK, CHUNK)
        load = pltpu.make_async_copy(mat.at[rows], own.at[rows], load_sem.at[k])
        load.start()
        loads.append(load)
    flip_in = pltpu.make_async_copy(flips_in, flips, flip_load.at[0])
    flip_in.start()
    slot = (z * RING + b) * RING + a
    keep = pltpu.make_async_copy(picks, picked.at[slot], pick_local.at[0])
    keep.start()

    @pl.when(core == 0)
    def _():
        pl.semaphore_wait(barrier, 1 + len(plane))
        signal(go.at[0], partner)

    @pl.when(core == 1)
    def _():
        pl.semaphore_wait(go.at[0], 1)
        for device in column:
            signal(barrier, device)

    flip_copy = remote(flips_in, flips_par, flip_sems.at[0], flip_sems.at[1], partner)
    flip_copy.start()
    core_copies = []
    for k in range(CHUNKS):
        rows = pl.ds(k * CHUNK, CHUNK)
        copy = remote(mat.at[rows], par.at[rows], core_send.at[k], core_recv.at[k], partner)
        copy.start()
        core_copies.append(copy)

    picks_a = [
        remote(picks, picked.at[slot], pick_send.at[k - 1], pick_recv.at[k - 1], peer_a(k)) for k in range(1, RING)
    ]

    @pl.when(core == 0)
    def _():
        for copy in picks_a:
            copy.start()
        for device in plane:
            signal(ready, device)
        pl.semaphore_wait(ready, len(plane))
        signal(go.at[1], partner)

    @pl.when(core == 1)
    def _():
        pl.semaphore_wait(go.at[1], 1)
        for copy in picks_a:
            copy.start()

    had[...] = hadamard_block()

    def transformed(block, values, flip_ref, sign):
        negative = jnp.concatenate([flip_ref[pl.ds(2 * block, 1), :], flip_ref[pl.ds(2 * block + 1, 1), :]], axis=1)
        signs = ((1 - 2 * negative).astype(F32) * sign).astype(BF16)
        high = values.astype(BF16)
        low = (values - high.astype(F32)).astype(BF16)
        both = jnp.concatenate([high, low], axis=1)
        product = jnp.dot(had[...] * signs, both, preferred_element_type=F32)
        return product[:, :COLS] + product[:, COLS:]

    own_sign = parity_sign(core, core)
    par_sign = jnp.float32(1.0)
    flip_in.wait()
    for k in range(CHUNKS):
        loads[k].wait()
        for j in range(CHUNK // BLOCK):
            block = k * (CHUNK // BLOCK) + j
            rows = pl.ds(block * BLOCK, BLOCK)
            mixed[rows, :] = transformed(block, own[rows, :], flips, own_sign)

    def fold(k):
        core_copies[k].wait()
        for j in range(CHUNK // BLOCK):
            block = k * (CHUNK // BLOCK) + j
            rows = pl.ds(block * BLOCK, BLOCK)
            mixed[rows, :] += transformed(block, par[rows, :], flips_par, par_sign)

    keep.wait()
    for copy in picks_a:
        copy.wait()
    picks_b = []
    line = pl.ds((z * RING + b) * RING, RING)
    for k in range(1, RING):
        copy = remote(picked.at[line], picked.at[line], pick_send.at[k + 2], pick_recv.at[k + 2], peer_b(k))
        copy.start()
        picks_b.append(copy)

    @pl.when(core == 1)
    def _():
        pl.semaphore_wait(barrier, len(column))
        signal(go.at[2], partner)

    @pl.when(core == 0)
    def _():
        pl.semaphore_wait(go.at[2], 1)

    flip_copy.wait()
    for k in range(2):
        fold(k)
    for copy in picks_b:
        copy.wait()
    picks_z = []
    layer = pl.ds(z * RING * RING, RING * RING)
    for k in (4, 3, 5, 2, 6, 1, 7):
        copy = remote(picked.at[layer], picked.at[layer], pick_send.at[k + 5], pick_recv.at[k + 5], peer_z(k))
        copy.start()
        picks_z.append((k, copy))
    for k in range(2, CHUNKS):
        fold(k)

    def butterfly(i, carry):
        values = [mixed[pl.ds(j * BLOCK + pl.multiple_of(i * 8, 8), 8), :] for j in range(BLOCKS)]
        span = 1
        while span < BLOCKS:
            after = list(values)
            for j in range(BLOCKS):
                if not j & span:
                    after[j] = values[j] + values[j + span]
                    after[j + span] = values[j] - values[j + span]
            values = after
            span *= 2
        for j in range(BLOCKS):
            mixed[pl.ds(j * BLOCK + pl.multiple_of(i * 8, 8), 8), :] = values[j]
        return carry

    lax.fori_loop(0, BLOCK // 8, butterfly, 0)

    scalar_copies = []

    def to_scalar(by):
        part = pl.ds(turn(z, by, DEPTH) * (RING * RING), RING * RING)
        copy = pltpu.make_async_copy(picked.at[part], picked_s.at[part], scalar_sem.at[by])
        copy.start()
        scalar_copies.append(copy)

    to_scalar(0)
    for k, copy in reversed(picks_z):
        copy.wait()
        to_scalar(DEPTH - k)
    for copy in scalar_copies:
        copy.wait()

    def gather(dst, base, dest, half):
        sign = parity_sign(dest, a)

        def body(q, carry):
            b_to = half * (RING // 2) + lax.div(q, DEPTH)
            z_to = lax.rem(q, DEPTH)
            place = (z_to * RING + b_to) * RING + dest
            for g in range(PER // 16):
                rows = [mixed[pl.ds(picked_s[place, 0, g * 16 + s], 1), :] for s in range(16)]
                for s in range(16):
                    dst[pl.ds(base + q * PER + g * 16 + s, 1), :] = rows[s] * sign
            return carry

        lax.fori_loop(0, RING // 2 * DEPTH, body, 0)

    right, left = peer_a(1), peer_a(RING - 1)
    at_right, at_left, at_opp = turn(a, 1, RING), turn(a, 3, RING), turn(a, 2, RING)

    def send_a(k, dst, device):
        copy = remote(out_a.at[k], dst, a_send.at[k], a_recv.at[k], device)
        copy.start()
        return copy

    gather(out_a.at[0], 0, at_opp, 0)
    c0 = send_a(0, opp_a.at[0], right)
    gather(out_a.at[1], 0, at_opp, 1)
    c1 = send_a(1, opp_a.at[1], left)
    gather(out_a.at[2], 0, at_right, 1)
    c2 = send_a(2, from_left_a.at[1], right)
    gather(out_a.at[3], 0, at_left, 0)
    c3 = send_a(3, from_right_a.at[0], left)
    gather(out_a.at[4], 0, at_right, 0)
    c0.wait_recv()
    out_a[4] += opp_a[0]
    c4 = send_a(4, from_left_a.at[0], right)
    gather(out_a.at[5], 0, at_left, 1)
    c1.wait_recv()
    out_a[5] += opp_a[1]
    c5 = send_a(5, from_right_a.at[1], left)
    gather(tot_a, 0, a, 0)
    gather(tot_a, PART_A, a, 1)
    c2.wait_recv()
    c3.wait_recv()

    def total_a(half):
        for j in range(RING // 2):
            b_to = half * (RING // 2) + j
            rows = pl.ds(b_to * 2 * PART_B, 2 * PART_B)
            inner = pl.ds(j * 2 * PART_B, 2 * PART_B)
            summed = tot_a[rows, :] + from_left_a[half, inner, :] + from_right_a[half, inner, :]
            tot_a[rows, :] = summed * parity_sign(jnp.int32(b_to), b)

    c4.wait_recv()
    total_a(0)
    c5.wait_recv()
    total_a(1)

    b_right, b_left, b_opp = turn(b, 1, RING), turn(b, 3, RING), turn(b, 2, RING)
    right_b, left_b = peer_b(1), peer_b(RING - 1)

    def rows_b(dest, half):
        return pl.ds(pl.multiple_of(dest * (2 * PART_B) + half * PART_B, 8), PART_B)

    def send_b(k, src, dst, device):
        copy = remote(src, dst, b_send.at[k], b_recv.at[k], device)
        copy.start()
        return copy

    d0 = send_b(0, tot_a.at[rows_b(b_opp, 0)], opp_b.at[0], right_b)
    d1 = send_b(1, tot_a.at[rows_b(b_opp, 1)], opp_b.at[1], left_b)
    d2 = send_b(2, tot_a.at[rows_b(b_right, 1)], from_left_b.at[1], right_b)
    d3 = send_b(3, tot_a.at[rows_b(b_left, 0)], from_right_b.at[0], left_b)
    d0.wait_recv()
    out_b[0] = tot_a[rows_b(b_right, 0), :] + opp_b[0]
    d4 = send_b(4, out_b.at[0], from_left_b.at[0], right_b)
    d1.wait_recv()
    out_b[1] = tot_a[rows_b(b_left, 1), :] + opp_b[1]
    d5 = send_b(5, out_b.at[1], from_right_b.at[1], left_b)
    d2.wait_recv()
    d3.wait_recv()

    def total_b(half):
        for j in range(DEPTH // 2):
            z_to = half * (DEPTH // 2) + j
            inner = pl.ds(j * PER, PER)
            own_rows = pl.ds(pl.multiple_of(b * (2 * PART_B) + z_to * PER, 8), PER)
            summed = tot_a[own_rows, :] + from_left_b[half, inner, :] + from_right_b[half, inner, :]
            tot_b[z_to] = summed * parity_sign(jnp.int32(z_to), z)

    d4.wait_recv()
    total_b(0)
    d5.wait_recv()
    total_b(1)

    z_copies = []
    for k in (4, 3, 5, 2, 6, 1, 7):
        copy = remote(tot_b.at[turn(z, k, DEPTH)], got_z.at[k - 1], z_send.at[k - 1], z_recv.at[k - 1], peer_z(k))
        copy.start()
        z_copies.append(copy)
    for copy in z_copies:
        copy.wait_recv()
    rows = tot_b[z]
    for k in range(DEPTH - 1):
        rows = rows + got_z[k]
    rows = rows * (1.0 / 1024.0)
    sketch[...] = rows

    part_g[...] = lax.dot_general(
        rows, rows, (((0,), (0,)), ((), ())), precision=lax.Precision.HIGHEST, preferred_element_type=F32
    )

    def send_g(k, src, dst, device):
        copy = remote(src, dst, g_send.at[k], g_recv.at[k], device)
        copy.start()
        return copy

    def piece(position):
        return pl.ds(pl.multiple_of(position * PIECE, PIECE), PIECE)

    copies = [send_g(k - 1, part_g.at[piece(turn(a, k, RING))], got_ga.at[k - 1], peer_a(k)) for k in range(1, RING)]
    for copy in copies:
        copy.wait_recv()
    piece_b[b] = part_g[piece(a), :] + got_ga[0] + got_ga[1] + got_ga[2]
    pending = copies
    copies = [send_g(k + 2, piece_b.at[b], piece_b.at[b], peer_b(k)) for k in range(1, RING)]
    for copy in copies:
        copy.wait_recv()
    piece_z[z] = piece_b[0] + piece_b[1] + piece_b[2] + piece_b[3]
    pending = pending + copies
    copies = [send_g(k + 5, piece_z.at[z], piece_z.at[z], peer_z(k)) for k in (4, 3, 5, 2, 6, 1, 7)]
    for copy in copies:
        copy.wait_recv()
    total = piece_z[0]
    for k in range(1, DEPTH):
        total = total + piece_z[k]
    full_g[piece(a), :] = total
    pending = pending + copies
    copies = [send_g(k + 12, full_g.at[piece(a)], full_g.at[piece(a)], peer_a(k)) for k in range(1, RING)]
    for copy in copies:
        copy.wait_recv()
    pending = pending + copies
    last = send_g(16, full_g, other_g, partner)
    last.wait_recv()
    gram[...] = (full_g[...] + other_g[...]) * (1.0 / (PER * 2 * RING * RING * DEPTH))
    pending = pending + [last]

    for copy in [c0, c1, c2, c3, c4, c5, d0, d1, d2, d3, d4, d5] + z_copies + pending:
        copy.wait_send()


def cholesky_kernel(gram, factor, work, upper):
    work[...] = gram[...]
    row = lax.broadcasted_iota(jnp.int32, (PANEL, COLS), 0)
    lane = lax.broadcasted_iota(jnp.int32, (PANEL, COLS), 1)
    for base in range(0, COLS, PANEL):
        panel = work[pl.ds(base, PANEL), :]
        columns = [jnp.broadcast_to(panel[:, base + k : base + k + 1], (PANEL, COLS)) for k in range(PANEL)]
        pivots = jnp.ones((PANEL, COLS), F32)
        for j in range(PANEL):
            pivot = columns[j][j : j + 1, :]
            pivots = jnp.where(row == j, columns[j], pivots)
            factors = jnp.where(row > j, columns[j] * (1.0 / pivot), 0.0)
            for k in range(j + 1, PANEL):
                columns[k] = columns[k] - factors * columns[k][j : j + 1, :]
            panel = panel - factors * panel[j : j + 1, :]
        root = lax.rsqrt(pivots)
        root = root * (1.5 - 0.5 * pivots * root * root)
        scaled = jnp.where(lane >= base + row, panel * root, 0.0)
        upper[pl.ds(base, PANEL), :] = scaled
        if base + PANEL < COLS:
            high = scaled.astype(BF16)
            rest = scaled - high.astype(F32)
            mid = rest.astype(BF16)
            low = (rest - mid.astype(F32)).astype(BF16)
            first = jnp.concatenate([high, high, mid, high, low, mid], axis=0)
            second = jnp.concatenate([high, mid, high, low, high, mid], axis=0)
            update = lax.dot_general(first, second, (((0,), (0,)), ((), ())), preferred_element_type=F32)
            after = base + PANEL
            work[pl.ds(after, COLS - after), :] -= update[after:, :]
    factor[...] = upper[...].T


def shards(matrix, flips, picks):
    vmem = pl.BlockSpec(memory_space=pltpu.VMEM)
    half_a = (PART_A, COLS)
    half_b = (PART_B, COLS)
    dma = pltpu.SemaphoreType.DMA
    sketch, gram = pl.pallas_call(
        kernel,
        name="blendenpik",
        out_shape=(
            jax.ShapeDtypeStruct((PER, COLS), F32),
            jax.ShapeDtypeStruct((COLS, COLS), F32),
        ),
        in_specs=[pl.BlockSpec(memory_space=pltpu.HBM)] * 3,
        out_specs=(vmem, vmem),
        scratch_shapes=[
            pltpu.VMEM((ROWS, COLS), F32),
            pltpu.VMEM((ROWS, COLS), F32),
            pltpu.VMEM((ROWS // COLS, COLS), jnp.int32),
            pltpu.VMEM((ROWS // COLS, COLS), jnp.int32),
            pltpu.VMEM((BLOCK, BLOCK), BF16),
            pltpu.VMEM((ROWS, COLS), F32),
            pltpu.VMEM((RING * RING * DEPTH, 1, PER), jnp.int32),
            pltpu.SMEM((RING * RING * DEPTH, 1, PER), jnp.int32),
            pltpu.VMEM((6, *half_a), F32),
            pltpu.VMEM((2, *half_a), F32),
            pltpu.VMEM((2, *half_a), F32),
            pltpu.VMEM((2, *half_a), F32),
            pltpu.VMEM((2 * PART_A, COLS), F32),
            pltpu.VMEM((2, *half_b), F32),
            pltpu.VMEM((2, *half_b), F32),
            pltpu.VMEM((2, *half_b), F32),
            pltpu.VMEM((2, *half_b), F32),
            pltpu.VMEM((DEPTH, PER, COLS), F32),
            pltpu.VMEM((DEPTH - 1, PER, COLS), F32),
            pltpu.VMEM((COLS, COLS), F32),
            pltpu.VMEM((RING - 1, PIECE, COLS), F32),
            pltpu.VMEM((RING, PIECE, COLS), F32),
            pltpu.VMEM((DEPTH, PIECE, COLS), F32),
            pltpu.VMEM((COLS, COLS), F32),
            pltpu.VMEM((COLS, COLS), F32),
            dma((CHUNKS,)),
            dma((1,)),
            pltpu.SemaphoreType.REGULAR((3,)),
            pltpu.SemaphoreType.REGULAR,
            dma((CHUNKS,)),
            dma((CHUNKS,)),
            dma((2,)),
            dma((13,)),
            dma((13,)),
            dma((1,)),
            dma((DEPTH,)),
            dma((6,)),
            dma((6,)),
            dma((6,)),
            dma((6,)),
            dma((7,)),
            dma((7,)),
            dma((17,)),
            dma((17,)),
        ],
        compiler_params=pltpu.CompilerParams(
            collective_id=0, has_side_effects=True, vmem_limit_bytes=48 * 1024 * 1024
        ),
    )(matrix, flips.reshape(ROWS // COLS, COLS), picks.reshape(1, PER))
    factor = pl.pallas_call(
        cholesky_kernel,
        name="factor",
        out_shape=jax.ShapeDtypeStruct((COLS, COLS), F32),
        in_specs=[vmem],
        out_specs=vmem,
        scratch_shapes=[pltpu.VMEM((COLS, COLS), F32)] * 2,
    )(gram)
    return (sketch, factor)


def solution(mesh):
    placed = (P("rows", None), P("rows"), P("rows"))
    return jax.shard_map(
        shards, mesh=mesh, in_specs=placed, out_specs=(P("rows", None), P()), check_vma=False
    )
```

```python
import jax
import jax.numpy as jnp
from jax import lax
from jax.experimental import pallas as pl
from jax.experimental.pallas import tpu as pltpu
from jax.sharding import PartitionSpec as P

MESH = pl.DeviceIdType.MESH
F32 = jnp.float32
BF16 = jnp.bfloat16

RING = 4
DEPTH = 8
ROWS = 4096
COLS = 128
PER = 64
BLOCK = 256
BLOCKS = ROWS // BLOCK
CHUNKS = 8
CHUNK = ROWS // CHUNKS
LAG = 2
PIECE = COLS // RING
PANEL = 16


def parity_sign(left, right):
    both = left & right
    both = (both ^ (both >> 1) ^ (both >> 2)) & 1
    return (1 - 2 * both).astype(F32)


def hadamard_block():
    row = lax.broadcasted_iota(jnp.int32, (BLOCK, BLOCK), 0)
    col = lax.broadcasted_iota(jnp.int32, (BLOCK, BLOCK), 1)
    both = row & col
    both = both ^ (both >> 4)
    both = both ^ (both >> 2)
    both = both ^ (both >> 1)
    return (1 - 2 * (both & 1)).astype(F32).astype(BF16)


def kernel(
    mat, flips_in, picks, sketch, gram,
    own, par, flips, flips_par, had, mixed, picked, picked_s,
    out_a, opp_a, from_left_a, from_right_a, tot_a,
    out_b, opp_b, from_left_b, from_right_b, tot_b,
    got_z, part_g, got_ga, piece_b, piece_z, full_g, other_g,
    load_sem, flip_load, go, ready, core_send, core_recv, flip_sems, pick_send, pick_recv, pick_local, scalar_sem,
    a_send, a_recv, b_send, b_recv, z_send, z_recv, g_send, g_recv,
):
    me = lax.axis_index("rows")
    core = lax.rem(me, 2)
    ypos = lax.rem(lax.div(me, 2), RING)
    xpos = lax.rem(lax.div(me, 2 * RING), RING)
    z = lax.div(me, 2 * RING * RING)
    a = ypos + core * (xpos - ypos)
    b = xpos + core * (ypos - xpos)
    step_a = 2 + core * (2 * RING - 2)
    step_b = 2 * RING - core * (2 * RING - 2)
    partner = me + 1 - 2 * core

    def turn(position, by, size):
        return lax.rem(position + by, size)

    def peer_a(by):
        return me + (turn(a, by, RING) - a) * step_a

    def peer_b(by):
        return me + (turn(b, by, RING) - b) * step_b

    def peer_z(by):
        return me + (turn(z, by, DEPTH) - z) * (2 * RING * RING)

    def remote(src, dst, send, recv, device):
        return pltpu.make_async_remote_copy(
            src_ref=src, dst_ref=dst, send_sem=send, recv_sem=recv,
            device_id=(device,), device_id_type=MESH,
        )

    barrier = pltpu.get_barrier_semaphore()
    plane = [peer_a(k) for k in range(1, RING)] + [peer_b(k) for k in range(1, RING)]
    column = [peer_z(k) for k in range(1, DEPTH)]

    def signal(semaphore, device):
        pl.semaphore_signal(semaphore, inc=1, device_id=(device,), device_id_type=MESH)

    @pl.when(core == 0)
    def _():
        for device in plane:
            signal(barrier, device)

    @pl.when(core == 1)
    def _():
        signal(barrier, partner)

    loads = []
    for k in range(CHUNKS):
        rows = pl.ds(k * CHUNK, CHUNK)
        load = pltpu.make_async_copy(mat.at[rows], own.at[rows], load_sem.at[k])
        load.start()
        loads.append(load)
    flip_in = pltpu.make_async_copy(flips_in, flips, flip_load.at[0])
    flip_in.start()
    slot = (z * RING + b) * RING + a
    keep = pltpu.make_async_copy(picks, picked.at[slot], pick_local.at[0])
    keep.start()

    had[...] = hadamard_block()

    def transformed(block, values, flip_ref, sign):
        negative = jnp.concatenate([flip_ref[pl.ds(2 * block, 1), :], flip_ref[pl.ds(2 * block + 1, 1), :]], axis=1)
        signs = ((1 - 2 * negative).astype(F32) * sign).astype(BF16)
        high = values.astype(BF16)
        low = (values - high.astype(F32)).astype(BF16)
        both = jnp.concatenate([high, low], axis=1)
        product = jnp.dot(had[...] * signs, both, preferred_element_type=F32)
        return product[:, :COLS] + product[:, COLS:]

    own_sign = parity_sign(core, core)
    par_sign = jnp.float32(1.0)
    flip_in.wait()
    for k in range(CHUNKS):
        loads[k].wait()
        for j in range(CHUNK // BLOCK):
            block = k * (CHUNK // BLOCK) + j
            rows = pl.ds(block * BLOCK, BLOCK)
            mixed[rows, :] = transformed(block, own[rows, :], flips, own_sign)

    @pl.when(core == 0)
    def _():
        pl.semaphore_wait(barrier, 1 + len(plane))
        signal(go.at[0], partner)

    @pl.when(core == 1)
    def _():
        pl.semaphore_wait(go.at[0], 1)
        for device in column:
            signal(barrier, device)

    flip_copy = remote(flips_in, flips_par, flip_sems.at[0], flip_sems.at[1], partner)
    flip_copy.start()
    core_copies = []
    for k in range(CHUNKS):
        rows = pl.ds(k * CHUNK, CHUNK)
        copy = remote(mat.at[rows], par.at[rows], core_send.at[k], core_recv.at[k], partner)
        copy.start()
        core_copies.append(copy)

    picks_a = [
        remote(picks, picked.at[slot], pick_send.at[k - 1], pick_recv.at[k - 1], peer_a(k)) for k in range(1, RING)
    ]

    @pl.when(core == 0)
    def _():
        for copy in picks_a:
            copy.start()
        for device in plane:
            signal(ready, device)
        pl.semaphore_wait(ready, len(plane))
        signal(go.at[1], partner)

    @pl.when(core == 1)
    def _():
        pl.semaphore_wait(go.at[1], 1)
        for copy in picks_a:
            copy.start()

    def fold(k):
        core_copies[k].wait()
        for j in range(CHUNK // BLOCK):
            block = k * (CHUNK // BLOCK) + j
            rows = pl.ds(block * BLOCK, BLOCK)
            mixed[rows, :] += transformed(block, par[rows, :], flips_par, par_sign)

    keep.wait()
    for copy in picks_a:
        copy.wait()
    picks_b = []
    line = pl.ds((z * RING + b) * RING, RING)
    for k in range(1, RING):
        copy = remote(picked.at[line], picked.at[line], pick_send.at[k + 2], pick_recv.at[k + 2], peer_b(k))
        copy.start()
        picks_b.append(copy)

    @pl.when(core == 1)
    def _():
        pl.semaphore_wait(barrier, len(column))
        signal(go.at[2], partner)

    @pl.when(core == 0)
    def _():
        pl.semaphore_wait(go.at[2], 1)

    flip_copy.wait()
    for k in range(2):
        fold(k)
    for copy in picks_b:
        copy.wait()
    layer = pl.ds(z * RING * RING, RING * RING)

    def picks_z(by):
        return remote(
            picked.at[layer], picked.at[layer], pick_send.at[6 + by], pick_recv.at[6 + by],
            peer_z(DEPTH - by),
        )

    for by in (1, 7, 2, 6, 3, 5, 4):
        picks_z(by).start()
    for k in range(2, CHUNKS):
        fold(k)

    def butterfly(i, carry):
        values = [mixed[pl.ds(j * BLOCK + pl.multiple_of(i * 8, 8), 8), :] for j in range(BLOCKS)]
        span = 1
        while span < BLOCKS:
            after = list(values)
            for j in range(BLOCKS):
                if not j & span:
                    after[j] = values[j] + values[j + span]
                    after[j + span] = values[j] - values[j + span]
            values = after
            span *= 2
        for j in range(BLOCKS):
            mixed[pl.ds(j * BLOCK + pl.multiple_of(i * 8, 8), 8), :] = values[j]
        return carry

    lax.fori_loop(0, BLOCK // 8, butterfly, 0)

    def offset(j):
        pair = lax.div(j, 2)
        return (pair + 1 + lax.rem(j, 2) * (6 - 2 * pair)) * (1 - lax.div(j, DEPTH - 1))

    def picks_to_scalar(j):
        part = pl.ds(turn(z, offset(j), DEPTH) * (RING * RING), RING * RING)
        return pltpu.make_async_copy(picked.at[part], picked_s.at[part], scalar_sem.at[j])

    def fetch(j):
        @pl.when(j < DEPTH - 1)
        def _():
            by = offset(j)
            remote(
                picked.at[layer], picked.at[layer], pick_send.at[6 + by], pick_recv.at[6 + by], peer_z(by)
            ).wait_recv()

        picks_to_scalar(j).start()

    def gather(j, k, dest, half):
        sign = parity_sign(dest, a)
        z_to = turn(z, offset(j), DEPTH)

        def body(q, carry):
            place = (z_to * RING + half * (RING // 2) + q) * RING + dest
            for g in range(PER // 16):
                rows = [mixed[pl.ds(picked_s[place, 0, g * 16 + s], 1), :] for s in range(16)]
                for s in range(16):
                    out_a[j, k, pl.ds(q * PER + g * 16 + s, 1), :] = rows[s] * sign
            return carry

        lax.fori_loop(0, RING // 2, body, 0)

    right, left = peer_a(1), peer_a(RING - 1)
    at_right, at_left, at_opp = turn(a, 1, RING), turn(a, 3, RING), turn(a, 2, RING)
    b_right, b_left, b_opp = turn(b, 1, RING), turn(b, 3, RING), turn(b, 2, RING)
    right_b, left_b = peer_b(1), peer_b(RING - 1)

    def copy_a(j, k):
        dst = (
            opp_a.at[j, 0], opp_a.at[j, 1], from_left_a.at[j, 1],
            from_right_a.at[j, 0], from_left_a.at[j, 0], from_right_a.at[j, 1],
        )[k]
        return remote(out_a.at[j, k], dst, a_send.at[j, k], a_recv.at[j, k], left if k % 2 else right)

    low, high = pl.ds(0, PER // 2), pl.ds(PER // 2, PER // 2)

    def copy_b(j, k):
        src, dst = (
            (tot_a.at[j, b_opp, low], opp_b.at[j, 0]),
            (tot_a.at[j, b_opp, high], opp_b.at[j, 1]),
            (tot_a.at[j, b_right, high], from_left_b.at[j, 1]),
            (tot_a.at[j, b_left, low], from_right_b.at[j, 0]),
            (out_b.at[j, 0], from_left_b.at[j, 0]),
            (out_b.at[j, 1], from_right_b.at[j, 1]),
        )[k]
        return remote(src, dst, b_send.at[j, k], b_recv.at[j, k], left_b if k % 2 else right_b)

    def copy_z(j):
        return remote(tot_b.at[j], got_z.at[j], z_send.at[j], z_recv.at[j], peer_z(offset(j)))

    def first(j):
        picks_to_scalar(j).wait()
        for k, dest, half in ((0, at_opp, 0), (1, at_opp, 1), (2, at_right, 1), (3, at_left, 0)):
            gather(j, k, dest, half)
            copy_a(j, k).start()
        for k, dest, half in ((4, at_right, 0), (5, at_left, 1), (6, a, 0), (7, a, 1)):
            gather(j, k, dest, half)

        @pl.when(j + 1 < DEPTH)
        def _():
            fetch(j + 1)

    def second(j):
        for k in (0, 1):
            copy_a(j, k).wait_recv()
            out_a[j, 4 + k] += opp_a[j, k]
            copy_a(j, 4 + k).start()

    def third(j):
        for k in (2, 3, 4, 5):
            copy_a(j, k).wait_recv()
        for b_to in range(RING):
            half, inner = b_to // 2, pl.ds(b_to % 2 * PER, PER)
            summed = out_a[j, 6 + half, inner, :] + from_left_a[j, half, inner, :] + from_right_a[j, half, inner, :]
            tot_a[j, b_to] = summed * parity_sign(jnp.int32(b_to), b)
        for k in range(4):
            copy_b(j, k).start()

    def fourth(j):
        copy_b(j, 0).wait_recv()
        out_b[j, 0] = tot_a[j, b_right, low, :] + opp_b[j, 0]
        copy_b(j, 4).start()
        copy_b(j, 1).wait_recv()
        out_b[j, 1] = tot_a[j, b_left, high, :] + opp_b[j, 1]
        copy_b(j, 5).start()

    def fifth(j):
        for k in (2, 3, 4, 5):
            copy_b(j, k).wait_recv()
        sign = parity_sign(turn(z, offset(j), DEPTH), z)
        for half, rows in ((0, low), (1, high)):
            tot_b[j, rows, :] = (tot_a[j, b, rows, :] + from_left_b[j, half] + from_right_b[j, half]) * sign

        @pl.when(j < DEPTH - 1)
        def _():
            copy_z(j).start()

    fetch(jnp.int32(0))

    def step(i, carry):
        for late, stage in enumerate((first, second, third, fourth, fifth)):
            j = i - LAG * late

            @pl.when((j >= 0) & (j < DEPTH))
            def _():
                stage(j)

        return carry

    lax.fori_loop(0, DEPTH + 4 * LAG, step, 0)

    def collect(j, rows):
        copy_z(j).wait_recv()
        return rows + got_z[j]

    rows = lax.fori_loop(0, DEPTH - 1, collect, tot_b[DEPTH - 1])
    rows = rows * (1.0 / 1024.0)
    sketch[...] = rows

    part_g[...] = lax.dot_general(
        rows, rows, (((0,), (0,)), ((), ())), precision=lax.Precision.HIGHEST, preferred_element_type=F32
    )

    def send_g(k, src, dst, device):
        copy = remote(src, dst, g_send.at[k], g_recv.at[k], device)
        copy.start()
        return copy

    def piece(position):
        return pl.ds(pl.multiple_of(position * PIECE, PIECE), PIECE)

    copies = [send_g(k - 1, part_g.at[piece(turn(a, k, RING))], got_ga.at[k - 1], peer_a(k)) for k in range(1, RING)]
    for copy in copies:
        copy.wait_recv()
    piece_b[b] = part_g[piece(a), :] + got_ga[0] + got_ga[1] + got_ga[2]
    pending = copies
    copies = [send_g(k + 2, piece_b.at[b], piece_b.at[b], peer_b(k)) for k in range(1, RING)]
    for copy in copies:
        copy.wait_recv()
    piece_z[z] = piece_b[0] + piece_b[1] + piece_b[2] + piece_b[3]
    pending = pending + copies
    copies = [send_g(k + 5, piece_z.at[z], piece_z.at[z], peer_z(k)) for k in (4, 3, 5, 2, 6, 1, 7)]
    for copy in copies:
        copy.wait_recv()
    total = piece_z[0]
    for k in range(1, DEPTH):
        total = total + piece_z[k]
    full_g[piece(a), :] = total
    pending = pending + copies
    copies = [send_g(k + 12, full_g.at[piece(a)], full_g.at[piece(a)], peer_a(k)) for k in range(1, RING)]
    for copy in copies:
        copy.wait_recv()
    pending = pending + copies
    last = send_g(16, full_g, other_g, partner)
    last.wait_recv()
    gram[...] = (full_g[...] + other_g[...]) * (1.0 / (PER * 2 * RING * RING * DEPTH))
    pending = pending + [last]

    def drain(j, carry):
        for k in range(6):
            copy_a(j, k).wait_send()
            copy_b(j, k).wait_send()

        @pl.when(j < DEPTH - 1)
        def _():
            copy_z(j).wait_send()
            picks_z(j + 1).wait_send()

        return carry

    lax.fori_loop(0, DEPTH, drain, 0)
    for copy in pending:
        copy.wait_send()


def cholesky_kernel(gram, factor, work, upper):
    work[...] = gram[...]
    row = lax.broadcasted_iota(jnp.int32, (PANEL, COLS), 0)
    lane = lax.broadcasted_iota(jnp.int32, (PANEL, COLS), 1)
    for base in range(0, COLS, PANEL):
        panel = work[pl.ds(base, PANEL), :]
        columns = [jnp.broadcast_to(panel[:, base + k : base + k + 1], (PANEL, COLS)) for k in range(PANEL)]
        pivots = jnp.ones((PANEL, COLS), F32)
        for j in range(PANEL):
            pivot = columns[j][j : j + 1, :]
            pivots = jnp.where(row == j, columns[j], pivots)
            factors = jnp.where(row > j, columns[j] * (1.0 / pivot), 0.0)
            for k in range(j + 1, PANEL):
                columns[k] = columns[k] - factors * columns[k][j : j + 1, :]
            panel = panel - factors * panel[j : j + 1, :]
        root = lax.rsqrt(pivots)
        root = root * (1.5 - 0.5 * pivots * root * root)
        scaled = jnp.where(lane >= base + row, panel * root, 0.0)
        upper[pl.ds(base, PANEL), :] = scaled
        if base + PANEL < COLS:
            high = scaled.astype(BF16)
            rest = scaled - high.astype(F32)
            mid = rest.astype(BF16)
            low = (rest - mid.astype(F32)).astype(BF16)
            first = jnp.concatenate([high, high, mid, high, low, mid], axis=0)
            second = jnp.concatenate([high, mid, high, low, high, mid], axis=0)
            update = lax.dot_general(first, second, (((0,), (0,)), ((), ())), preferred_element_type=F32)
            after = base + PANEL
            work[pl.ds(after, COLS - after), :] -= update[after:, :]
    factor[...] = upper[...].T


def shards(matrix, flips, picks):
    vmem = pl.BlockSpec(memory_space=pltpu.VMEM)
    half_a = (DEPTH, 2, RING // 2 * PER, COLS)
    half_b = (DEPTH, 2, PER // 2, COLS)
    dma = pltpu.SemaphoreType.DMA
    sketch, gram = pl.pallas_call(
        kernel,
        name="blendenpik",
        out_shape=(
            jax.ShapeDtypeStruct((PER, COLS), F32),
            jax.ShapeDtypeStruct((COLS, COLS), F32),
        ),
        in_specs=[pl.BlockSpec(memory_space=pltpu.HBM)] * 3,
        out_specs=(vmem, vmem),
        scratch_shapes=[
            pltpu.VMEM((ROWS, COLS), F32),
            pltpu.VMEM((ROWS, COLS), F32),
            pltpu.VMEM((ROWS // COLS, COLS), jnp.int32),
            pltpu.VMEM((ROWS // COLS, COLS), jnp.int32),
            pltpu.VMEM((BLOCK, BLOCK), BF16),
            pltpu.VMEM((ROWS, COLS), F32),
            pltpu.VMEM((RING * RING * DEPTH, 1, PER), jnp.int32),
            pltpu.SMEM((RING * RING * DEPTH, 1, PER), jnp.int32),
            pltpu.VMEM((DEPTH, 8, RING // 2 * PER, COLS), F32),
            pltpu.VMEM(half_a, F32),
            pltpu.VMEM(half_a, F32),
            pltpu.VMEM(half_a, F32),
            pltpu.VMEM((DEPTH, RING, PER, COLS), F32),
            pltpu.VMEM(half_b, F32),
            pltpu.VMEM(half_b, F32),
            pltpu.VMEM(half_b, F32),
            pltpu.VMEM(half_b, F32),
            pltpu.VMEM((DEPTH, PER, COLS), F32),
            pltpu.VMEM((DEPTH - 1, PER, COLS), F32),
            pltpu.VMEM((COLS, COLS), F32),
            pltpu.VMEM((RING - 1, PIECE, COLS), F32),
            pltpu.VMEM((RING, PIECE, COLS), F32),
            pltpu.VMEM((DEPTH, PIECE, COLS), F32),
            pltpu.VMEM((COLS, COLS), F32),
            pltpu.VMEM((COLS, COLS), F32),
            dma((CHUNKS,)),
            dma((1,)),
            pltpu.SemaphoreType.REGULAR((3,)),
            pltpu.SemaphoreType.REGULAR,
            dma((CHUNKS,)),
            dma((CHUNKS,)),
            dma((2,)),
            dma((14,)),
            dma((14,)),
            dma((1,)),
            dma((DEPTH,)),
            dma((DEPTH, 6)),
            dma((DEPTH, 6)),
            dma((DEPTH, 6)),
            dma((DEPTH, 6)),
            dma((7,)),
            dma((7,)),
            dma((17,)),
            dma((17,)),
        ],
        compiler_params=pltpu.CompilerParams(
            collective_id=0, has_side_effects=True, vmem_limit_bytes=67043328
        ),
    )(matrix, flips.reshape(ROWS // COLS, COLS), picks.reshape(1, PER))
    factor = pl.pallas_call(
        cholesky_kernel,
        name="factor",
        out_shape=jax.ShapeDtypeStruct((COLS, COLS), F32),
        in_specs=[vmem],
        out_specs=vmem,
        scratch_shapes=[pltpu.VMEM((COLS, COLS), F32)] * 2,
    )(gram)
    return (sketch, factor)


def solution(mesh):
    placed = (P("rows", None), P("rows"), P("rows"))
    return jax.shard_map(
        shards, mesh=mesh, in_specs=placed, out_specs=(P("rows", None), P()), check_vma=False
    )
```

```python
import jax
import jax.numpy as jnp
from jax import lax
from jax.experimental import pallas as pl
from jax.experimental.pallas import tpu as pltpu
from jax.sharding import PartitionSpec as P

MESH = pl.DeviceIdType.MESH
F32 = jnp.float32
BF16 = jnp.bfloat16

RING = 4
DEPTH = 8
ROWS = 4096
COLS = 128
PER = 64
BLOCK = 256
BLOCKS = ROWS // BLOCK
CHUNKS = 8
CHUNK = ROWS // CHUNKS
LAG = 2
ORDER = (0, 1, 6, 4, 3, 5, 2, 7)
PIECE = COLS // (RING * RING)
PANEL = 16


def parity_sign(left, right):
    both = left & right
    both = (both ^ (both >> 1) ^ (both >> 2)) & 1
    return (1 - 2 * both).astype(F32)


def hadamard_block():
    row = lax.broadcasted_iota(jnp.int32, (BLOCK, BLOCK), 0)
    col = lax.broadcasted_iota(jnp.int32, (BLOCK, BLOCK), 1)
    both = row & col
    both = both ^ (both >> 4)
    both = both ^ (both >> 2)
    both = both ^ (both >> 1)
    return (1 - 2 * (both & 1)).astype(F32).astype(BF16)


def exact_product(rows):
    high = rows.astype(BF16)
    rest = rows - high.astype(F32)
    mid = rest.astype(BF16)
    low = (rest - mid.astype(F32)).astype(BF16)
    first = jnp.concatenate([high, high, mid, high, low, mid], axis=0)
    second = jnp.concatenate([high, mid, high, low, high, mid], axis=0)
    return lax.dot_general(first, second, (((0,), (0,)), ((), ())), preferred_element_type=F32)


def kernel(
    mat, flips_in, picks, sketch, gram,
    own, par, flips, flips_par, had, mixed, picked, picked_s,
    out_a, opp_a, from_left_a, from_right_a, tot_a,
    out_b, opp_b, from_left_b, from_right_b, tot_b,
    got_z, part_g, got_g, piece_z, full_g, other_g,
    load_sem, flip_load, go, ready, core_send, core_recv, flip_sems, pick_send, pick_recv, pick_local, scalar_sem,
    a_send, a_recv, b_send, b_recv, z_send, z_recv, g_send, g_recv,
):
    me = lax.axis_index("rows")
    core = lax.rem(me, 2)
    ypos = lax.rem(lax.div(me, 2), RING)
    xpos = lax.rem(lax.div(me, 2 * RING), RING)
    z = lax.div(me, 2 * RING * RING)
    a = ypos + core * (xpos - ypos)
    b = xpos + core * (ypos - xpos)
    step_a = 2 + core * (2 * RING - 2)
    step_b = 2 * RING - core * (2 * RING - 2)
    partner = me + 1 - 2 * core

    def turn(position, by, size):
        return lax.rem(position + by, size)

    def peer_a(by):
        return me + (turn(a, by, RING) - a) * step_a

    def peer_b(by):
        return me + (turn(b, by, RING) - b) * step_b

    def peer_z(by):
        return me + (turn(z, by, DEPTH) - z) * (2 * RING * RING)

    def remote(src, dst, send, recv, device):
        return pltpu.make_async_remote_copy(
            src_ref=src, dst_ref=dst, send_sem=send, recv_sem=recv,
            device_id=(device,), device_id_type=MESH,
        )

    barrier = pltpu.get_barrier_semaphore()
    plane = [peer_a(k) for k in range(1, RING)] + [peer_b(k) for k in range(1, RING)]
    column = [peer_z(k) for k in range(1, DEPTH)]

    def signal(semaphore, device):
        pl.semaphore_signal(semaphore, inc=1, device_id=(device,), device_id_type=MESH)

    @pl.when(core == 0)
    def _():
        for device in plane:
            signal(barrier, device)

    @pl.when(core == 1)
    def _():
        signal(barrier, partner)

    loads = []
    for k in range(CHUNKS):
        rows = pl.ds(k * CHUNK, CHUNK)
        load = pltpu.make_async_copy(mat.at[rows], own.at[rows], load_sem.at[k])
        load.start()
        loads.append(load)
    flip_in = pltpu.make_async_copy(flips_in, flips, flip_load.at[0])
    flip_in.start()
    slot = (z * RING + b) * RING + a
    keep = pltpu.make_async_copy(picks, picked.at[slot], pick_local.at[0])
    keep.start()

    @pl.when(core == 0)
    def _():
        pl.semaphore_wait(barrier, 1 + len(plane))
        signal(go.at[0], partner)

    @pl.when(core == 1)
    def _():
        pl.semaphore_wait(go.at[0], 1)
        for device in column:
            signal(barrier, device)

    flip_copy = remote(flips_in, flips_par, flip_sems.at[0], flip_sems.at[1], partner)
    flip_copy.start()
    core_copies = []
    for k in range(CHUNKS):
        rows = pl.ds(k * CHUNK, CHUNK)
        copy = remote(mat.at[rows], par.at[rows], core_send.at[k], core_recv.at[k], partner)
        copy.start()
        core_copies.append(copy)

    picks_a = [
        remote(picks, picked.at[slot], pick_send.at[k - 1], pick_recv.at[k - 1], peer_a(k)) for k in range(1, RING)
    ]

    @pl.when(core == 0)
    def _():
        for copy in picks_a:
            copy.start()
        for device in plane:
            signal(ready, device)
        pl.semaphore_wait(ready, len(plane))
        signal(go.at[1], partner)

    @pl.when(core == 1)
    def _():
        pl.semaphore_wait(go.at[1], 1)
        for copy in picks_a:
            copy.start()

    had[...] = hadamard_block()

    def transformed(block, values, flip_ref, sign):
        negative = jnp.concatenate([flip_ref[pl.ds(2 * block, 1), :], flip_ref[pl.ds(2 * block + 1, 1), :]], axis=1)
        signs = ((1 - 2 * negative).astype(F32) * sign).astype(BF16)
        high = values.astype(BF16)
        low = (values - high.astype(F32)).astype(BF16)
        both = jnp.concatenate([high, low], axis=1)
        product = jnp.dot(had[...] * signs, both, preferred_element_type=F32)
        return product[:, :COLS] + product[:, COLS:]

    own_sign = parity_sign(core, core)
    par_sign = jnp.float32(1.0)
    flip_in.wait()
    for k in range(CHUNKS):
        loads[k].wait()
        for j in range(CHUNK // BLOCK):
            block = k * (CHUNK // BLOCK) + j
            rows = pl.ds(block * BLOCK, BLOCK)
            mixed[rows, :] = transformed(block, own[rows, :], flips, own_sign)

    def fold(k):
        core_copies[k].wait()
        for j in range(CHUNK // BLOCK):
            block = k * (CHUNK // BLOCK) + j
            rows = pl.ds(block * BLOCK, BLOCK)
            mixed[rows, :] += transformed(block, par[rows, :], flips_par, par_sign)

    flip_copy.wait()
    for k in range(2):
        fold(k)
    keep.wait()
    for copy in picks_a:
        copy.wait()
    picks_b = []
    line = pl.ds((z * RING + b) * RING, RING)
    for k in range(1, RING):
        copy = remote(picked.at[line], picked.at[line], pick_send.at[k + 2], pick_recv.at[k + 2], peer_b(k))
        copy.start()
        picks_b.append(copy)
    for k in range(2, 6):
        fold(k)
    for copy in picks_b:
        copy.wait()

    @pl.when(core == 1)
    def _():
        pl.semaphore_wait(barrier, len(column))
        signal(go.at[2], partner)

    @pl.when(core == 0)
    def _():
        pl.semaphore_wait(go.at[2], 1)

    layer = pl.ds(z * RING * RING, RING * RING)

    def picks_z(by):
        return remote(
            picked.at[layer], picked.at[layer], pick_send.at[6 + by], pick_recv.at[6 + by],
            peer_z(DEPTH - by),
        )

    for by in (1, 6, 4, 3, 5, 2, 7):
        picks_z(by).start()
    for k in range(6, CHUNKS):
        fold(k)

    def butterfly(i, carry):
        values = [mixed[pl.ds(j * BLOCK + pl.multiple_of(i * 8, 8), 8), :] for j in range(BLOCKS)]
        span = 1
        while span < BLOCKS:
            after = list(values)
            for j in range(BLOCKS):
                if not j & span:
                    after[j] = values[j] + values[j + span]
                    after[j + span] = values[j] - values[j + span]
            values = after
            span *= 2
        for j in range(BLOCKS):
            mixed[pl.ds(j * BLOCK + pl.multiple_of(i * 8, 8), 8), :] = values[j]
        return carry

    lax.fori_loop(0, BLOCK // 8, butterfly, 0)

    def offset(j):
        place = ORDER[0]
        for k in range(1, DEPTH):
            place = place + (ORDER[k] - ORDER[k - 1]) * lax.div(j + DEPTH - k, DEPTH)
        return place

    def picks_to_scalar(j):
        part = pl.ds(turn(z, offset(j), DEPTH) * (RING * RING), RING * RING)
        return pltpu.make_async_copy(picked.at[part], picked_s.at[part], scalar_sem.at[j])

    def fetch(j):
        @pl.when(j > 0)
        def _():
            by = offset(j)
            remote(
                picked.at[layer], picked.at[layer], pick_send.at[6 + by], pick_recv.at[6 + by], peer_z(by)
            ).wait_recv()

        picks_to_scalar(j).start()

    def gather(j, k, dest, half):
        sign = parity_sign(dest, a)
        z_to = turn(z, offset(j), DEPTH)

        def body(q, carry):
            place = (z_to * RING + half * (RING // 2) + q) * RING + dest
            for g in range(PER // 16):
                rows = [mixed[pl.ds(picked_s[place, 0, g * 16 + s], 1), :] for s in range(16)]
                for s in range(16):
                    out_a[j, k, pl.ds(q * PER + g * 16 + s, 1), :] = rows[s] * sign
            return carry

        lax.fori_loop(0, RING // 2, body, 0)

    right, left = peer_a(1), peer_a(RING - 1)
    at_right, at_left, at_opp = turn(a, 1, RING), turn(a, 3, RING), turn(a, 2, RING)
    b_right, b_left, b_opp = turn(b, 1, RING), turn(b, 3, RING), turn(b, 2, RING)
    right_b, left_b = peer_b(1), peer_b(RING - 1)

    def copy_a(j, k):
        dst = (
            opp_a.at[j, 0], opp_a.at[j, 1], from_left_a.at[j, 1],
            from_right_a.at[j, 0], from_left_a.at[j, 0], from_right_a.at[j, 1],
        )[k]
        return remote(out_a.at[j, k], dst, a_send.at[j, k], a_recv.at[j, k], left if k % 2 else right)

    low, high = pl.ds(0, PER // 2), pl.ds(PER // 2, PER // 2)

    def copy_b(j, k):
        src, dst = (
            (tot_a.at[j, b_opp, low], opp_b.at[j, 0]),
            (tot_a.at[j, b_opp, high], opp_b.at[j, 1]),
            (tot_a.at[j, b_right, high], from_left_b.at[j, 1]),
            (tot_a.at[j, b_left, low], from_right_b.at[j, 0]),
            (out_b.at[j, 0], from_left_b.at[j, 0]),
            (out_b.at[j, 1], from_right_b.at[j, 1]),
        )[k]
        return remote(src, dst, b_send.at[j, k], b_recv.at[j, k], left_b if k % 2 else right_b)

    def copy_z(j):
        return remote(tot_b.at[j], got_z.at[j], z_send.at[j], z_recv.at[j], peer_z(offset(j)))

    def first(j):
        picks_to_scalar(j).wait()
        for k, dest, half in ((0, at_opp, 0), (1, at_opp, 1), (2, at_right, 1), (3, at_left, 0)):
            gather(j, k, dest, half)
            copy_a(j, k).start()
        for k, dest, half in ((4, at_right, 0), (5, at_left, 1), (6, a, 0), (7, a, 1)):
            gather(j, k, dest, half)

        @pl.when(j + 1 < DEPTH)
        def _():
            fetch(j + 1)

    def second(j):
        for k in (0, 1):
            copy_a(j, k).wait_recv()
            out_a[j, 4 + k] += opp_a[j, k]
            copy_a(j, 4 + k).start()

    def third(j):
        for k in (2, 3, 4, 5):
            copy_a(j, k).wait_recv()
        for b_to in range(RING):
            half, inner = b_to // 2, pl.ds(b_to % 2 * PER, PER)
            summed = out_a[j, 6 + half, inner, :] + from_left_a[j, half, inner, :] + from_right_a[j, half, inner, :]
            tot_a[j, b_to] = summed * parity_sign(jnp.int32(b_to), b)
        for k in range(4):
            copy_b(j, k).start()

    def fourth(j):
        copy_b(j, 0).wait_recv()
        out_b[j, 0] = tot_a[j, b_right, low, :] + opp_b[j, 0]
        copy_b(j, 4).start()
        copy_b(j, 1).wait_recv()
        out_b[j, 1] = tot_a[j, b_left, high, :] + opp_b[j, 1]
        copy_b(j, 5).start()

    def fifth(j):
        for k in (2, 3, 4, 5):
            copy_b(j, k).wait_recv()
        sign = parity_sign(turn(z, offset(j), DEPTH), z)
        for half, rows in ((0, low), (1, high)):
            tot_b[j, rows, :] = (tot_a[j, b, rows, :] + from_left_b[j, half] + from_right_b[j, half]) * sign

        @pl.when(j > 0)
        def _():
            copy_z(j).start()

    fetch(jnp.int32(0))

    def step(i, carry):
        for late, stage in enumerate((first, second, third, fourth, fifth)):
            j = i - LAG * late

            @pl.when((j >= 0) & (j < DEPTH))
            def _():
                stage(j)

        return carry

    lax.fori_loop(0, DEPTH + 4 * LAG, step, 0)

    def collect(j, rows):
        copy_z(j).wait_recv()
        return rows + got_z[j]

    rows = lax.fori_loop(1, DEPTH, collect, tot_b[0])
    rows = rows * (1.0 / 1024.0)
    sketch[...] = rows

    part_g[...] = exact_product(rows)

    def send_g(k, src, dst, device):
        copy = remote(src, dst, g_send.at[k], g_recv.at[k], device)
        copy.start()
        return copy

    def piece(at_a, at_b):
        return pl.ds(pl.multiple_of((at_a * RING + at_b) * PIECE, PIECE), PIECE)

    turns = [(da, db) for da in range(RING) for db in range(RING)]
    turns.sort(key=lambda t: -min(t[0], RING - t[0]) - min(t[1], RING - t[1]))
    pending = []
    for da, db in turns[:-1]:
        to_a, to_b = turn(a, da, RING), turn(b, db, RING)
        k = da * RING + db
        pending.append(send_g(
            k, part_g.at[piece(to_a, to_b)], got_g.at[k], me + (to_a - a) * step_a + (to_b - b) * step_b
        ))
    total = part_g[piece(a, b), :]
    for copy in pending:
        copy.wait_recv()
    for k in range(1, RING * RING):
        total = total + got_g[k]
    piece_z[z] = total
    copies = [send_g(15 + k, piece_z.at[z], piece_z.at[z], peer_z(k)) for k in (4, 3, 5, 2, 6, 1, 7)]
    for copy in copies:
        copy.wait_recv()
    pending = pending + copies
    total = piece_z[0]
    for k in range(1, DEPTH):
        total = total + piece_z[k]
    full_g[piece(a, b), :] = total
    mine = full_g.at[piece(a, b)]
    copies = []
    for da, db in turns:
        k = da * RING + db
        there = me + (turn(a, da, RING) - a) * step_a + (turn(b, db, RING) - b) * step_b
        copies.append(send_g(38 + k, mine, other_g.at[piece(a, b)], there + 1 - 2 * core))
        if k:
            copies.append(send_g(22 + k, mine, mine, there))
    for copy in copies:
        copy.wait_recv()
    pending = pending + copies
    gram[...] = (full_g[...] + other_g[...]) * (1.0 / (PER * 2 * RING * RING * DEPTH))

    def drain(j, carry):
        for k in range(6):
            copy_a(j, k).wait_send()
            copy_b(j, k).wait_send()

        @pl.when(j > 0)
        def _():
            copy_z(j).wait_send()
            picks_z(j).wait_send()

        return carry

    lax.fori_loop(0, DEPTH, drain, 0)
    for copy in pending:
        copy.wait_send()


def cholesky_kernel(gram, sketch_in, factor, sketch, work, upper, rows, sems):
    fetch = pltpu.make_async_copy(sketch_in, rows, sems.at[0])
    fetch.start()
    work[...] = gram[...]
    row = lax.broadcasted_iota(jnp.int32, (PANEL, COLS), 0)
    lane = lax.broadcasted_iota(jnp.int32, (PANEL, COLS), 1)
    fetch.wait()
    store = pltpu.make_async_copy(rows, sketch, sems.at[1])
    store.start()
    for base in range(0, COLS, PANEL):
        panel = work[pl.ds(base, PANEL), :]
        columns = [jnp.broadcast_to(panel[:, base + k : base + k + 1], (PANEL, COLS)) for k in range(PANEL)]
        pivots = jnp.ones((PANEL, COLS), F32)
        for j in range(PANEL):
            pivot = columns[j][j : j + 1, :]
            pivots = jnp.where(row == j, columns[j], pivots)
            factors = jnp.where(row > j, columns[j] * (1.0 / pivot), 0.0)
            for k in range(j + 1, PANEL):
                columns[k] = columns[k] - factors * columns[k][j : j + 1, :]
            panel = panel - factors * panel[j : j + 1, :]
        root = lax.rsqrt(pivots)
        root = root * (1.5 - 0.5 * pivots * root * root)
        scaled = jnp.where(lane >= base + row, panel * root, 0.0)
        upper[pl.ds(base, PANEL), :] = scaled
        if base + PANEL < COLS:
            update = exact_product(scaled)
            after = base + PANEL
            work[pl.ds(after, COLS - after), :] -= update[after:, :]
    factor[...] = upper[...].T
    store.wait()


def shards(matrix, flips, picks):
    vmem = pl.BlockSpec(memory_space=pltpu.VMEM)
    half_a = (DEPTH, 2, RING // 2 * PER, COLS)
    half_b = (DEPTH, 2, PER // 2, COLS)
    dma = pltpu.SemaphoreType.DMA
    sketch, gram = pl.pallas_call(
        kernel,
        name="blendenpik",
        out_shape=(
            jax.ShapeDtypeStruct((PER, COLS), F32),
            jax.ShapeDtypeStruct((COLS, COLS), F32),
        ),
        in_specs=[pl.BlockSpec(memory_space=pltpu.HBM)] * 3,
        out_specs=(vmem, vmem),
        scratch_shapes=[
            pltpu.VMEM((ROWS, COLS), F32),
            pltpu.VMEM((ROWS, COLS), F32),
            pltpu.VMEM((ROWS // COLS, COLS), jnp.int32),
            pltpu.VMEM((ROWS // COLS, COLS), jnp.int32),
            pltpu.VMEM((BLOCK, BLOCK), BF16),
            pltpu.VMEM((ROWS, COLS), F32),
            pltpu.VMEM((RING * RING * DEPTH, 1, PER), jnp.int32),
            pltpu.SMEM((RING * RING * DEPTH, 1, PER), jnp.int32),
            pltpu.VMEM((DEPTH, 8, RING // 2 * PER, COLS), F32),
            pltpu.VMEM(half_a, F32),
            pltpu.VMEM(half_a, F32),
            pltpu.VMEM(half_a, F32),
            pltpu.VMEM((DEPTH, RING, PER, COLS), F32),
            pltpu.VMEM(half_b, F32),
            pltpu.VMEM(half_b, F32),
            pltpu.VMEM(half_b, F32),
            pltpu.VMEM(half_b, F32),
            pltpu.VMEM((DEPTH, PER, COLS), F32),
            pltpu.VMEM((DEPTH, PER, COLS), F32),
            pltpu.VMEM((COLS, COLS), F32),
            pltpu.VMEM((RING * RING, PIECE, COLS), F32),
            pltpu.VMEM((DEPTH, PIECE, COLS), F32),
            pltpu.VMEM((COLS, COLS), F32),
            pltpu.VMEM((COLS, COLS), F32),
            dma((CHUNKS,)),
            dma((1,)),
            pltpu.SemaphoreType.REGULAR((3,)),
            pltpu.SemaphoreType.REGULAR,
            dma((CHUNKS,)),
            dma((CHUNKS,)),
            dma((2,)),
            dma((14,)),
            dma((14,)),
            dma((1,)),
            dma((DEPTH,)),
            dma((DEPTH, 6)),
            dma((DEPTH, 6)),
            dma((DEPTH, 6)),
            dma((DEPTH, 6)),
            dma((DEPTH,)),
            dma((DEPTH,)),
            dma((54,)),
            dma((54,)),
        ],
        compiler_params=pltpu.CompilerParams(
            collective_id=0, has_side_effects=True, vmem_limit_bytes=67043328
        ),
    )(matrix, flips.reshape(ROWS // COLS, COLS), picks.reshape(1, PER))
    hbm = pl.BlockSpec(memory_space=pltpu.HBM)
    factor, sketch = pl.pallas_call(
        cholesky_kernel,
        name="factor",
        out_shape=(jax.ShapeDtypeStruct((COLS, COLS), F32), jax.ShapeDtypeStruct((PER, COLS), F32)),
        in_specs=[vmem, hbm],
        out_specs=(vmem, hbm),
        scratch_shapes=[
            pltpu.VMEM((COLS, COLS), F32),
            pltpu.VMEM((COLS, COLS), F32),
            pltpu.VMEM((PER, COLS), F32),
            dma((2,)),
        ],
    )(gram, sketch)
    return (sketch, factor)


def solution(mesh):
    placed = (P("rows", None), P("rows"), P("rows"))
    return jax.shard_map(
        shards, mesh=mesh, in_specs=placed, out_specs=(P("rows", None), P()), check_vma=False
    )
```

```python
import jax
import jax.numpy as jnp
from jax import lax
from jax.experimental import pallas as pl
from jax.experimental.pallas import tpu as pltpu
from jax.sharding import PartitionSpec as P

MESH = pl.DeviceIdType.MESH
F32 = jnp.float32
BF16 = jnp.bfloat16

RING = 4
DEPTH = 8
ROWS = 4096
COLS = 128
PER = 64
BLOCK = 256
BLOCKS = ROWS // BLOCK
CHUNKS = 8
CHUNK = ROWS // CHUNKS
LAG = 2
ORDER = (0, 4, 5, 3, 6, 2, 7, 1)
PIECE = COLS // (RING * RING)
PANEL = 16


def parity_sign(left, right):
    both = left & right
    both = (both ^ (both >> 1) ^ (both >> 2)) & 1
    return (1 - 2 * both).astype(F32)


def hadamard_block():
    row = lax.broadcasted_iota(jnp.int32, (BLOCK, BLOCK), 0)
    col = lax.broadcasted_iota(jnp.int32, (BLOCK, BLOCK), 1)
    both = row & col
    both = both ^ (both >> 4)
    both = both ^ (both >> 2)
    both = both ^ (both >> 1)
    return (1 - 2 * (both & 1)).astype(F32).astype(BF16)


def exact_product(rows):
    high = rows.astype(BF16)
    rest = rows - high.astype(F32)
    mid = rest.astype(BF16)
    low = (rest - mid.astype(F32)).astype(BF16)
    first = jnp.concatenate([high, high, mid, high, low, mid], axis=0)
    second = jnp.concatenate([high, mid, high, low, high, mid], axis=0)
    return lax.dot_general(first, second, (((0,), (0,)), ((), ())), preferred_element_type=F32)


def kernel(
    mat, flips_in, picks, sketch, gram,
    own, par, flips, flips_par, had, mixed, picked, picked_s,
    out_a, opp_a, from_left_a, from_right_a, tot_a,
    got_z, tot_z, got_b, part_g, got_g, piece_z, full_g, other_g,
    load_sem, flip_load, go, ready, core_send, core_recv, flip_sems, pick_send, pick_recv, pick_local, scalar_sem,
    a_send, a_recv, b_send, b_recv, z_send, z_recv, g_send, g_recv,
):
    me = lax.axis_index("rows")
    core = lax.rem(me, 2)
    ypos = lax.rem(lax.div(me, 2), RING)
    xpos = lax.rem(lax.div(me, 2 * RING), RING)
    z = lax.div(me, 2 * RING * RING)
    a = ypos + core * (xpos - ypos)
    b = xpos + core * (ypos - xpos)
    step_a = 2 + core * (2 * RING - 2)
    step_b = 2 * RING - core * (2 * RING - 2)
    partner = me + 1 - 2 * core

    def turn(position, by, size):
        return lax.rem(position + by, size)

    def peer_a(by):
        return me + (turn(a, by, RING) - a) * step_a

    def peer_b(by):
        return me + (turn(b, by, RING) - b) * step_b

    def peer_z(by):
        return me + (turn(z, by, DEPTH) - z) * (2 * RING * RING)

    def remote(src, dst, send, recv, device):
        return pltpu.make_async_remote_copy(
            src_ref=src, dst_ref=dst, send_sem=send, recv_sem=recv,
            device_id=(device,), device_id_type=MESH,
        )

    barrier = pltpu.get_barrier_semaphore()
    plane = [peer_a(k) for k in range(1, RING)] + [peer_b(k) for k in range(1, RING)]
    column = [peer_z(k) for k in range(1, DEPTH)]

    def signal(semaphore, device):
        pl.semaphore_signal(semaphore, inc=1, device_id=(device,), device_id_type=MESH)

    @pl.when(core == 0)
    def _():
        for device in plane:
            signal(barrier, device)

    @pl.when(core == 1)
    def _():
        signal(barrier, partner)

    loads = []
    for k in range(CHUNKS):
        rows = pl.ds(k * CHUNK, CHUNK)
        load = pltpu.make_async_copy(mat.at[rows], own.at[rows], load_sem.at[k])
        load.start()
        loads.append(load)
    flip_in = pltpu.make_async_copy(flips_in, flips, flip_load.at[0])
    flip_in.start()
    slot = (z * RING + b) * RING + a
    keep = pltpu.make_async_copy(picks, picked.at[slot], pick_local.at[0])
    keep.start()

    @pl.when(core == 0)
    def _():
        pl.semaphore_wait(barrier, 1 + len(plane))
        signal(go.at[0], partner)

    @pl.when(core == 1)
    def _():
        pl.semaphore_wait(go.at[0], 1)
        for device in column:
            signal(barrier, device)

    flip_copy = remote(flips_in, flips_par, flip_sems.at[0], flip_sems.at[1], partner)
    flip_copy.start()
    core_copies = []
    for k in range(CHUNKS):
        rows = pl.ds(k * CHUNK, CHUNK)
        copy = remote(mat.at[rows], par.at[rows], core_send.at[k], core_recv.at[k], partner)
        copy.start()
        core_copies.append(copy)

    picks_a = [
        remote(picks, picked.at[slot], pick_send.at[k - 1], pick_recv.at[k - 1], peer_a(k)) for k in range(1, RING)
    ]

    @pl.when(core == 0)
    def _():
        for copy in picks_a:
            copy.start()
        for device in plane:
            signal(ready, device)

    had[...] = hadamard_block()

    def transformed(block, values, flip_ref, sign):
        negative = jnp.concatenate([flip_ref[pl.ds(2 * block, 1), :], flip_ref[pl.ds(2 * block + 1, 1), :]], axis=1)
        signs = ((1 - 2 * negative).astype(F32) * sign).astype(BF16)
        high = values.astype(BF16)
        low = (values - high.astype(F32)).astype(BF16)
        both = jnp.concatenate([high, low], axis=1)
        product = jnp.dot(had[...] * signs, both, preferred_element_type=F32)
        return product[:, :COLS] + product[:, COLS:]

    own_sign = parity_sign(core, core)
    par_sign = jnp.float32(1.0)
    flip_in.wait()
    for k in range(CHUNKS):
        loads[k].wait()
        for j in range(CHUNK // BLOCK):
            block = k * (CHUNK // BLOCK) + j
            rows = pl.ds(block * BLOCK, BLOCK)
            mixed[rows, :] = transformed(block, own[rows, :], flips, own_sign)
        if k == 2:

            @pl.when(core == 0)
            def _():
                pl.semaphore_wait(ready, len(plane))
                signal(go.at[1], partner)

            @pl.when(core == 1)
            def _():
                pl.semaphore_wait(go.at[1], 1)
                for copy in picks_a:
                    copy.start()


    def fold(k):
        core_copies[k].wait()
        for j in range(CHUNK // BLOCK):
            block = k * (CHUNK // BLOCK) + j
            rows = pl.ds(block * BLOCK, BLOCK)
            mixed[rows, :] += transformed(block, par[rows, :], flips_par, par_sign)

    keep.wait()
    for copy in picks_a:
        copy.wait()
    picks_b = []
    line = pl.ds((z * RING + b) * RING, RING)
    for k in range(1, RING):
        copy = remote(picked.at[line], picked.at[line], pick_send.at[k + 2], pick_recv.at[k + 2], peer_b(k))
        copy.start()
        picks_b.append(copy)
    flip_copy.wait()
    for k in range(3):
        fold(k)
    for copy in picks_b:
        copy.wait()

    @pl.when(core == 1)
    def _():
        pl.semaphore_wait(barrier, len(column))
        signal(go.at[2], partner)

    @pl.when(core == 0)
    def _():
        pl.semaphore_wait(go.at[2], 1)

    layer = pl.ds(z * RING * RING, RING * RING)

    def picks_z(by):
        return remote(
            picked.at[layer], picked.at[layer], pick_send.at[6 + by], pick_recv.at[6 + by],
            peer_z(DEPTH - by),
        )

    for by in (4, 5, 3, 6, 2, 7, 1):
        picks_z(by).start()
    for k in range(3, CHUNKS):
        fold(k)

    def butterfly(i, carry):
        values = [mixed[pl.ds(j * BLOCK + pl.multiple_of(i * 8, 8), 8), :] for j in range(BLOCKS)]
        span = 1
        while span < BLOCKS:
            after = list(values)
            for j in range(BLOCKS):
                if not j & span:
                    after[j] = values[j] + values[j + span]
                    after[j + span] = values[j] - values[j + span]
            values = after
            span *= 2
        for j in range(BLOCKS):
            mixed[pl.ds(j * BLOCK + pl.multiple_of(i * 8, 8), 8), :] = values[j]
        return carry

    lax.fori_loop(0, BLOCK // 8, butterfly, 0)

    def offset(j):
        place = ORDER[0]
        for k in range(1, DEPTH):
            place = place + (ORDER[k] - ORDER[k - 1]) * lax.div(j + DEPTH - k, DEPTH)
        return place

    def picks_to_scalar(j):
        part = pl.ds(turn(z, offset(j), DEPTH) * (RING * RING), RING * RING)
        return pltpu.make_async_copy(picked.at[part], picked_s.at[part], scalar_sem.at[j])

    def fetch(j):
        @pl.when(j > 0)
        def _():
            by = offset(j)
            remote(
                picked.at[layer], picked.at[layer], pick_send.at[6 + by], pick_recv.at[6 + by], peer_z(by)
            ).wait_recv()

        picks_to_scalar(j).start()

    def gather(j, k, dest, half):
        sign = parity_sign(dest, a)
        z_to = turn(z, offset(j), DEPTH)

        def body(q, carry):
            place = (z_to * RING + half * (RING // 2) + q) * RING + dest
            for g in range(PER // 16):
                rows = [mixed[pl.ds(picked_s[place, 0, g * 16 + s], 1), :] for s in range(16)]
                for s in range(16):
                    out_a[j, k, pl.ds(q * PER + g * 16 + s, 1), :] = rows[s] * sign
            return carry

        lax.fori_loop(0, RING // 2, body, 0)

    right, left = peer_a(1), peer_a(RING - 1)
    at_right, at_left, at_opp = turn(a, 1, RING), turn(a, 3, RING), turn(a, 2, RING)

    def copy_a(j, k):
        dst = (
            opp_a.at[j, 0], opp_a.at[j, 1], from_left_a.at[j, 1],
            from_right_a.at[j, 0], from_left_a.at[j, 0], from_right_a.at[j, 1],
        )[k]
        return remote(out_a.at[j, k], dst, a_send.at[j, k], a_recv.at[j, k], left if k % 2 else right)

    def copy_z(j):
        ahead = turn(z, 1 + (DEPTH - 2) * (1 - lax.rem(j, 2)), DEPTH)
        return remote(tot_a.at[j], got_z.at[j], z_send.at[j], z_recv.at[j], me + (ahead - z) * (2 * RING * RING))

    def first(j):
        picks_to_scalar(j).wait()
        for k, dest, half in ((0, at_opp, 0), (1, at_opp, 1), (2, at_right, 1), (3, at_left, 0)):
            gather(j, k, dest, half)
            copy_a(j, k).start()
        for k, dest, half in ((4, at_right, 0), (5, at_left, 1), (6, a, 0), (7, a, 1)):
            gather(j, k, dest, half)

        @pl.when(j + 1 < DEPTH)
        def _():
            fetch(j + 1)

    def second(j):
        for k in (0, 1):
            copy_a(j, k).wait_recv()
            out_a[j, 4 + k] += opp_a[j, k]
            copy_a(j, 4 + k).start()

    def third(j):
        for k in (2, 3, 4, 5):
            copy_a(j, k).wait_recv()
        sign = parity_sign(turn(z, offset(j), DEPTH), z)
        for b_to in range(RING):
            half, inner = b_to // 2, pl.ds(b_to % 2 * PER, PER)
            summed = out_a[j, 6 + half, inner, :] + from_left_a[j, half, inner, :] + from_right_a[j, half, inner, :]
            tot_a[j, b_to] = summed * sign

        @pl.when(j > 2)
        def _():
            copy_z(j - 2).wait_recv()
            for b_to in range(RING):
                tot_a[j, b_to] += got_z[j - 2, b_to]

        @pl.when(j > 0)
        def _():
            copy_z(j).start()

    fetch(jnp.int32(0))

    def step(i, carry):
        for late, stage in enumerate((first, second, third)):
            j = i - LAG * late

            @pl.when((j >= 0) & (j < DEPTH))
            def _():
                stage(j)

        return carry

    lax.fori_loop(0, DEPTH + 2 * LAG, step, 0)

    for j in (DEPTH - 2, DEPTH - 1):
        copy_z(jnp.int32(j)).wait_recv()
    for b_to in range(RING):
        summed = tot_a[0, b_to] + got_z[DEPTH - 2, b_to] + got_z[DEPTH - 1, b_to]
        tot_z[b_to] = summed * parity_sign(jnp.int32(b_to), b)

    b_copies = []
    for k in (2, 1, 3):
        copy = remote(
            tot_z.at[turn(b, k, RING)], got_b.at[k - 1], b_send.at[k - 1], b_recv.at[k - 1], peer_b(k)
        )
        copy.start()
        b_copies.append(copy)
    for copy in b_copies:
        copy.wait_recv()
    rows = tot_z[b] + got_b[0] + got_b[1] + got_b[2]
    rows = rows * (1.0 / 1024.0)
    sketch[...] = rows

    part_g[...] = exact_product(rows)

    def send_g(k, src, dst, device):
        copy = remote(src, dst, g_send.at[k], g_recv.at[k], device)
        copy.start()
        return copy

    def piece(at_a, at_b):
        return pl.ds(pl.multiple_of((at_a * RING + at_b) * PIECE, PIECE), PIECE)

    turns = [(da, db) for da in range(RING) for db in range(RING)]
    turns.sort(key=lambda t: -min(t[0], RING - t[0]) - min(t[1], RING - t[1]))
    pending = []
    for da, db in turns[:-1]:
        to_a, to_b = turn(a, da, RING), turn(b, db, RING)
        k = da * RING + db
        pending.append(send_g(
            k, part_g.at[piece(to_a, to_b)], got_g.at[k], me + (to_a - a) * step_a + (to_b - b) * step_b
        ))
    def drain(j, carry):
        for k in range(6):
            copy_a(j, k).wait_send()

        @pl.when(j > 0)
        def _():
            copy_z(j).wait_send()
            picks_z(j).wait_send()

        return carry

    lax.fori_loop(0, DEPTH, drain, 0)
    for copy in b_copies:
        copy.wait_send()
    total = part_g[piece(a, b), :]
    for copy in pending:
        copy.wait_recv()
    for k in range(1, RING * RING):
        total = total + got_g[k]
    piece_z[z] = total
    copies = [send_g(15 + k, piece_z.at[z], piece_z.at[z], peer_z(k)) for k in (4, 3, 5, 2, 6, 1, 7)]
    for copy in copies:
        copy.wait_recv()
    pending = pending + copies
    total = piece_z[0]
    for k in range(1, DEPTH):
        total = total + piece_z[k]
    full_g[piece(a, b), :] = total
    mine = full_g.at[piece(a, b)]
    copies = []
    for da, db in turns:
        k = da * RING + db
        there = me + (turn(a, da, RING) - a) * step_a + (turn(b, db, RING) - b) * step_b
        copies.append(send_g(38 + k, mine, other_g.at[piece(a, b)], there + 1 - 2 * core))
        if k:
            copies.append(send_g(22 + k, mine, mine, there))
    for copy in pending:
        copy.wait_send()
    for copy in copies:
        copy.wait_recv()
    gram[...] = (full_g[...] + other_g[...]) * (1.0 / (PER * 2 * RING * RING * DEPTH))

    for copy in copies:
        copy.wait_send()


def cholesky_kernel(gram, sketch_in, factor, sketch, work, upper, rows, sems):
    fetch = pltpu.make_async_copy(sketch_in, rows, sems.at[0])
    fetch.start()
    work[...] = gram[...]
    row = lax.broadcasted_iota(jnp.int32, (PANEL, COLS), 0)
    lane = lax.broadcasted_iota(jnp.int32, (PANEL, COLS), 1)
    fetch.wait()
    store = pltpu.make_async_copy(rows, sketch, sems.at[1])
    store.start()
    for base in range(0, COLS, PANEL):
        panel = work[pl.ds(base, PANEL), :]
        columns = [jnp.broadcast_to(panel[:, base + k : base + k + 1], (PANEL, COLS)) for k in range(PANEL)]
        pivots = jnp.ones((PANEL, COLS), F32)
        for j in range(PANEL):
            pivot = columns[j][j : j + 1, :]
            pivots = jnp.where(row == j, columns[j], pivots)
            factors = jnp.where(row > j, columns[j] * (1.0 / pivot), 0.0)
            for k in range(j + 1, PANEL):
                columns[k] = columns[k] - factors * columns[k][j : j + 1, :]
            panel = panel - factors * panel[j : j + 1, :]
        root = lax.rsqrt(pivots)
        root = root * (1.5 - 0.5 * pivots * root * root)
        scaled = jnp.where(lane >= base + row, panel * root, 0.0)
        upper[pl.ds(base, PANEL), :] = scaled
        if base + PANEL < COLS:
            update = exact_product(scaled)
            after = base + PANEL
            work[pl.ds(after, COLS - after), :] -= update[after:, :]
    factor[...] = upper[...].T
    store.wait()


def shards(matrix, flips, picks):
    vmem = pl.BlockSpec(memory_space=pltpu.VMEM)
    half_a = (DEPTH, 2, RING // 2 * PER, COLS)
    dma = pltpu.SemaphoreType.DMA
    sketch, gram = pl.pallas_call(
        kernel,
        name="blendenpik",
        out_shape=(
            jax.ShapeDtypeStruct((PER, COLS), F32),
            jax.ShapeDtypeStruct((COLS, COLS), F32),
        ),
        in_specs=[pl.BlockSpec(memory_space=pltpu.HBM)] * 3,
        out_specs=(vmem, vmem),
        scratch_shapes=[
            pltpu.VMEM((ROWS, COLS), F32),
            pltpu.VMEM((ROWS, COLS), F32),
            pltpu.VMEM((ROWS // COLS, COLS), jnp.int32),
            pltpu.VMEM((ROWS // COLS, COLS), jnp.int32),
            pltpu.VMEM((BLOCK, BLOCK), BF16),
            pltpu.VMEM((ROWS, COLS), F32),
            pltpu.VMEM((RING * RING * DEPTH, 1, PER), jnp.int32),
            pltpu.SMEM((RING * RING * DEPTH, 1, PER), jnp.int32),
            pltpu.VMEM((DEPTH, 8, RING // 2 * PER, COLS), F32),
            pltpu.VMEM(half_a, F32),
            pltpu.VMEM(half_a, F32),
            pltpu.VMEM(half_a, F32),
            pltpu.VMEM((DEPTH, RING, PER, COLS), F32),
            pltpu.VMEM((DEPTH, RING, PER, COLS), F32),
            pltpu.VMEM((RING, PER, COLS), F32),
            pltpu.VMEM((RING - 1, PER, COLS), F32),
            pltpu.VMEM((COLS, COLS), F32),
            pltpu.VMEM((RING * RING, PIECE, COLS), F32),
            pltpu.VMEM((DEPTH, PIECE, COLS), F32),
            pltpu.VMEM((COLS, COLS), F32),
            pltpu.VMEM((COLS, COLS), F32),
            dma((CHUNKS,)),
            dma((1,)),
            pltpu.SemaphoreType.REGULAR((3,)),
            pltpu.SemaphoreType.REGULAR,
            dma((CHUNKS,)),
            dma((CHUNKS,)),
            dma((2,)),
            dma((14,)),
            dma((14,)),
            dma((1,)),
            dma((DEPTH,)),
            dma((DEPTH, 6)),
            dma((DEPTH, 6)),
            dma((3,)),
            dma((3,)),
            dma((DEPTH,)),
            dma((DEPTH,)),
            dma((54,)),
            dma((54,)),
        ],
        compiler_params=pltpu.CompilerParams(
            collective_id=0, has_side_effects=True, vmem_limit_bytes=67043328
        ),
    )(matrix, flips.reshape(ROWS // COLS, COLS), picks.reshape(1, PER))
    hbm = pl.BlockSpec(memory_space=pltpu.HBM)
    factor, sketch = pl.pallas_call(
        cholesky_kernel,
        name="factor",
        out_shape=(jax.ShapeDtypeStruct((COLS, COLS), F32), jax.ShapeDtypeStruct((PER, COLS), F32)),
        in_specs=[vmem, hbm],
        out_specs=(vmem, hbm),
        scratch_shapes=[
            pltpu.VMEM((COLS, COLS), F32),
            pltpu.VMEM((COLS, COLS), F32),
            pltpu.VMEM((PER, COLS), F32),
            dma((2,)),
        ],
    )(gram, sketch)
    return (sketch, factor)


def solution(mesh):
    placed = (P("rows", None), P("rows"), P("rows"))
    return jax.shard_map(
        shards, mesh=mesh, in_specs=placed, out_specs=(P("rows", None), P()), check_vma=False
    )
```

```python
import jax
import jax.numpy as jnp
from jax import lax
from jax.experimental import pallas as pl
from jax.experimental.pallas import tpu as pltpu
from jax.sharding import PartitionSpec as P

MESH = pl.DeviceIdType.MESH
F32 = jnp.float32
BF16 = jnp.bfloat16

RING = 4
DEPTH = 8
ROWS = 4096
COLS = 128
PER = 64
BLOCK = 256
BLOCKS = ROWS // BLOCK
CHUNKS = 8
CHUNK = ROWS // CHUNKS
ORDER = (0, 4, 5, 3, 6, 2, 7, 1)
PIECE = COLS // (RING * RING)
PANEL = 16


def parity_sign(left, right):
    both = left & right
    both = (both ^ (both >> 1) ^ (both >> 2)) & 1
    return (1 - 2 * both).astype(F32)


def hadamard_block():
    row = lax.broadcasted_iota(jnp.int32, (BLOCK, BLOCK), 0)
    col = lax.broadcasted_iota(jnp.int32, (BLOCK, BLOCK), 1)
    both = row & col
    both = both ^ (both >> 4)
    both = both ^ (both >> 2)
    both = both ^ (both >> 1)
    return (1 - 2 * (both & 1)).astype(F32).astype(BF16)


def exact_product(rows):
    high = rows.astype(BF16)
    rest = rows - high.astype(F32)
    mid = rest.astype(BF16)
    low = (rest - mid.astype(F32)).astype(BF16)
    first = jnp.concatenate([high, high, mid, high, low, mid], axis=0)
    second = jnp.concatenate([high, mid, high, low, high, mid], axis=0)
    return lax.dot_general(first, second, (((0,), (0,)), ((), ())), preferred_element_type=F32)


def kernel(
    mat, flips_in, picks, sketch, gram,
    own, par, flips, flips_par, had, mixed, picked, picked_s,
    out_a, opp_a, from_left_a, from_right_a, tot_a,
    got_z, tot_z, got_b, part_g, got_g, piece_z, full_g, other_g,
    load_sem, flip_load, go, ready, core_send, core_recv, flip_sems, pick_send, pick_recv, pick_local, scalar_sem,
    a_send, a_recv, b_send, b_recv, z_send, z_recv, g_send, g_recv,
):
    me = lax.axis_index("rows")
    core = lax.rem(me, 2)
    ypos = lax.rem(lax.div(me, 2), RING)
    xpos = lax.rem(lax.div(me, 2 * RING), RING)
    z = lax.div(me, 2 * RING * RING)
    a = ypos + core * (xpos - ypos)
    b = xpos + core * (ypos - xpos)
    step_a = 2 + core * (2 * RING - 2)
    step_b = 2 * RING - core * (2 * RING - 2)
    partner = me + 1 - 2 * core

    def turn(position, by, size):
        return lax.rem(position + by, size)

    def peer_a(by):
        return me + (turn(a, by, RING) - a) * step_a

    def peer_b(by):
        return me + (turn(b, by, RING) - b) * step_b

    def peer_z(by):
        return me + (turn(z, by, DEPTH) - z) * (2 * RING * RING)

    def remote(src, dst, send, recv, device):
        return pltpu.make_async_remote_copy(
            src_ref=src, dst_ref=dst, send_sem=send, recv_sem=recv,
            device_id=(device,), device_id_type=MESH,
        )

    barrier = pltpu.get_barrier_semaphore()
    plane = [peer_a(k) for k in range(1, RING)] + [peer_b(k) for k in range(1, RING)]
    column = [peer_z(k) for k in range(1, DEPTH)]

    def signal(semaphore, device):
        pl.semaphore_signal(semaphore, inc=1, device_id=(device,), device_id_type=MESH)

    @pl.when(core == 0)
    def _():
        for device in plane:
            signal(barrier, device)

    @pl.when(core == 1)
    def _():
        signal(barrier, partner)

    loads = []
    for k in range(CHUNKS):
        rows = pl.ds(k * CHUNK, CHUNK)
        load = pltpu.make_async_copy(mat.at[rows], own.at[rows], load_sem.at[k])
        load.start()
        loads.append(load)
    flip_in = pltpu.make_async_copy(flips_in, flips, flip_load.at[0])
    flip_in.start()
    slot = (z * RING + b) * RING + a
    keep = pltpu.make_async_copy(picks, picked.at[slot], pick_local.at[0])
    keep.start()

    @pl.when(core == 0)
    def _():
        pl.semaphore_wait(barrier, 1 + len(plane))
        signal(go.at[0], partner)

    @pl.when(core == 1)
    def _():
        pl.semaphore_wait(go.at[0], 1)
        for device in column:
            signal(barrier, device)

    flip_copy = remote(flips_in, flips_par, flip_sems.at[0], flip_sems.at[1], partner)
    flip_copy.start()
    core_copies = []
    for k in range(CHUNKS):
        rows = pl.ds(k * CHUNK, CHUNK)
        copy = remote(mat.at[rows], par.at[rows], core_send.at[k], core_recv.at[k], partner)
        copy.start()
        core_copies.append(copy)

    picks_a = [
        remote(picks, picked.at[slot], pick_send.at[k - 1], pick_recv.at[k - 1], peer_a(k)) for k in range(1, RING)
    ]

    @pl.when(core == 0)
    def _():
        for copy in picks_a:
            copy.start()
        for device in plane:
            signal(ready, device)

    had[...] = hadamard_block()

    def transformed(block, values, flip_ref, sign):
        negative = jnp.concatenate([flip_ref[pl.ds(2 * block, 1), :], flip_ref[pl.ds(2 * block + 1, 1), :]], axis=1)
        signs = ((1 - 2 * negative).astype(F32) * sign).astype(BF16)
        high = values.astype(BF16)
        low = (values - high.astype(F32)).astype(BF16)
        both = jnp.concatenate([high, low], axis=1)
        product = jnp.dot(had[...] * signs, both, preferred_element_type=F32)
        return product[:, :COLS] + product[:, COLS:]

    own_sign = parity_sign(core, core)
    par_sign = jnp.float32(1.0)
    flip_in.wait()
    for k in range(CHUNKS):
        loads[k].wait()
        for j in range(CHUNK // BLOCK):
            block = k * (CHUNK // BLOCK) + j
            rows = pl.ds(block * BLOCK, BLOCK)
            mixed[rows, :] = transformed(block, own[rows, :], flips, own_sign)
        if k == 2:

            @pl.when(core == 0)
            def _():
                pl.semaphore_wait(ready, len(plane))
                signal(go.at[1], partner)

            @pl.when(core == 1)
            def _():
                pl.semaphore_wait(go.at[1], 1)
                for copy in picks_a:
                    copy.start()


    def fold(k):
        core_copies[k].wait()
        for j in range(CHUNK // BLOCK):
            block = k * (CHUNK // BLOCK) + j
            rows = pl.ds(block * BLOCK, BLOCK)
            mixed[rows, :] += transformed(block, par[rows, :], flips_par, par_sign)

    keep.wait()
    for copy in picks_a:
        copy.wait()
    picks_b = []
    line = pl.ds((z * RING + b) * RING, RING)
    for k in range(1, RING):
        copy = remote(picked.at[line], picked.at[line], pick_send.at[k + 2], pick_recv.at[k + 2], peer_b(k))
        copy.start()
        picks_b.append(copy)
    flip_copy.wait()
    for k in range(3):
        fold(k)
    for copy in picks_b:
        copy.wait()

    @pl.when(core == 1)
    def _():
        pl.semaphore_wait(barrier, len(column))
        signal(go.at[2], partner)

    @pl.when(core == 0)
    def _():
        pl.semaphore_wait(go.at[2], 1)

    layer = pl.ds(z * RING * RING, RING * RING)

    def picks_z(by):
        return remote(
            picked.at[layer], picked.at[layer], pick_send.at[6 + by], pick_recv.at[6 + by],
            peer_z(DEPTH - by),
        )

    for by in (4, 5, 3, 6, 2, 7, 1):
        picks_z(by).start()
    for k in range(3, CHUNKS):
        fold(k)

    def butterfly(i, carry):
        values = [mixed[pl.ds(j * BLOCK + pl.multiple_of(i * 8, 8), 8), :] for j in range(BLOCKS)]
        span = 1
        while span < BLOCKS:
            after = list(values)
            for j in range(BLOCKS):
                if not j & span:
                    after[j] = values[j] + values[j + span]
                    after[j + span] = values[j] - values[j + span]
            values = after
            span *= 2
        for j in range(BLOCKS):
            mixed[pl.ds(j * BLOCK + pl.multiple_of(i * 8, 8), 8), :] = values[j]
        return carry

    lax.fori_loop(0, BLOCK // 8, butterfly, 0)

    def offset(j):
        place = ORDER[0]
        for k in range(1, DEPTH):
            place = place + (ORDER[k] - ORDER[k - 1]) * lax.div(j + DEPTH - k, DEPTH)
        return place

    def picks_to_scalar(j):
        part = pl.ds(turn(z, offset(j), DEPTH) * (RING * RING), RING * RING)
        return pltpu.make_async_copy(picked.at[part], picked_s.at[part], scalar_sem.at[j])

    def fetch(j):
        @pl.when(j > 0)
        def _():
            by = offset(j)
            remote(
                picked.at[layer], picked.at[layer], pick_send.at[6 + by], pick_recv.at[6 + by], peer_z(by)
            ).wait_recv()

        picks_to_scalar(j).start()

    def gather(j, k, dest, half):
        sign = parity_sign(dest, a)
        z_to = turn(z, offset(j), DEPTH)

        def body(q, carry):
            place = (z_to * RING + half * (RING // 2) + q) * RING + dest
            for g in range(PER // 16):
                rows = [mixed[pl.ds(picked_s[place, 0, g * 16 + s], 1), :] for s in range(16)]
                for s in range(16):
                    out_a[j, k, pl.ds(q * PER + g * 16 + s, 1), :] = rows[s] * sign
            return carry

        lax.fori_loop(0, RING // 2, body, 0)

    right, left = peer_a(1), peer_a(RING - 1)
    at_right, at_left, at_opp = turn(a, 1, RING), turn(a, 3, RING), turn(a, 2, RING)

    def copy_a(j, k):
        dst = (
            opp_a.at[j, 0], opp_a.at[j, 1], from_left_a.at[j, 1],
            from_right_a.at[j, 0], from_left_a.at[j, 0], from_right_a.at[j, 1],
        )[k]
        return remote(out_a.at[j, k], dst, a_send.at[j, k], a_recv.at[j, k], left if k % 2 else right)

    def copy_z(j):
        ahead = turn(z, 1 + (DEPTH - 2) * (1 - lax.rem(j, 2)), DEPTH)
        return remote(tot_a.at[j], got_z.at[j], z_send.at[j], z_recv.at[j], me + (ahead - z) * (2 * RING * RING))

    def first(j):
        @pl.when(j == 1)
        def _():
            fetch(j)

        picks_to_scalar(j).wait()
        for k, dest, half in ((0, at_opp, 0), (1, at_opp, 1), (2, at_right, 1), (3, at_left, 0)):
            gather(j, k, dest, half)
            copy_a(j, k).start()
        for k, dest, half in ((4, at_right, 0), (5, at_left, 1), (6, a, 0), (7, a, 1)):
            gather(j, k, dest, half)

        @pl.when((j > 0) & (j + 1 < DEPTH))
        def _():
            fetch(j + 1)

    def second(j):
        for k in (0, 1):
            copy_a(j, k).wait_recv()
            out_a[j, 4 + k] += opp_a[j, k]
            copy_a(j, 4 + k).start()

    def third(j):
        for k in (2, 3, 4, 5):
            copy_a(j, k).wait_recv()
        sign = parity_sign(turn(z, offset(j), DEPTH), z)
        for b_to in range(RING):
            half, inner = b_to // 2, pl.ds(b_to % 2 * PER, PER)
            summed = out_a[j, 6 + half, inner, :] + from_left_a[j, half, inner, :] + from_right_a[j, half, inner, :]
            tot_a[j, b_to] = summed * sign

        @pl.when(j > 2)
        def _():
            copy_z(j - 2).wait_recv()
            for b_to in range(RING):
                tot_a[j, b_to] += got_z[j - 2, b_to]

        @pl.when(j > 0)
        def _():
            copy_z(j).start()

    fetch(jnp.int32(0))

    def step(i, carry):
        for late, stage in ((1, second), (0, first), (3, third)):
            j = i - late

            @pl.when((j >= 0) & (j < DEPTH))
            def _():
                stage(j)

        return carry

    lax.fori_loop(0, DEPTH + 3, step, 0)

    for j in (DEPTH - 2, DEPTH - 1):
        copy_z(jnp.int32(j)).wait_recv()
    for b_to in range(RING):
        summed = tot_a[0, b_to] + got_z[DEPTH - 2, b_to] + got_z[DEPTH - 1, b_to]
        tot_z[b_to] = summed * parity_sign(jnp.int32(b_to), b)

    b_copies = []
    for k in (2, 1, 3):
        copy = remote(
            tot_z.at[turn(b, k, RING)], got_b.at[k - 1], b_send.at[k - 1], b_recv.at[k - 1], peer_b(k)
        )
        copy.start()
        b_copies.append(copy)
    for copy in b_copies:
        copy.wait_recv()
    rows = tot_z[b] + got_b[0] + got_b[1] + got_b[2]
    rows = rows * (1.0 / 1024.0)
    sketch[...] = rows

    part_g[...] = exact_product(rows)

    def send_g(k, src, dst, device):
        copy = remote(src, dst, g_send.at[k], g_recv.at[k], device)
        copy.start()
        return copy

    def piece(at_a, at_b):
        return pl.ds(pl.multiple_of((at_a * RING + at_b) * PIECE, PIECE), PIECE)

    turns = [(da, db) for da in range(RING) for db in range(RING)]
    turns.sort(key=lambda t: -min(t[0], RING - t[0]) - min(t[1], RING - t[1]))
    pending = []
    for da, db in turns[:-1]:
        to_a, to_b = turn(a, da, RING), turn(b, db, RING)
        k = da * RING + db
        pending.append(send_g(
            k, part_g.at[piece(to_a, to_b)], got_g.at[k], me + (to_a - a) * step_a + (to_b - b) * step_b
        ))
    def drain(j, carry):
        for k in range(6):
            copy_a(j, k).wait_send()

        @pl.when(j > 0)
        def _():
            copy_z(j).wait_send()
            picks_z(j).wait_send()

        return carry

    lax.fori_loop(0, DEPTH, drain, 0)
    for copy in b_copies:
        copy.wait_send()
    total = part_g[piece(a, b), :]
    for copy in pending:
        copy.wait_recv()
    for k in range(1, RING * RING):
        total = total + got_g[k]
    piece_z[z] = total
    copies = [send_g(15 + k, piece_z.at[z], piece_z.at[z], peer_z(k)) for k in (4, 3, 5, 2, 6, 1, 7)]
    for copy in copies:
        copy.wait_recv()
    pending = pending + copies
    total = piece_z[0]
    for k in range(1, DEPTH):
        total = total + piece_z[k]
    full_g[piece(a, b), :] = total
    mine = full_g.at[piece(a, b)]
    copies = []
    for da, db in turns:
        k = da * RING + db
        there = me + (turn(a, da, RING) - a) * step_a + (turn(b, db, RING) - b) * step_b
        copies.append(send_g(38 + k, mine, other_g.at[piece(a, b)], there + 1 - 2 * core))
        if k:
            copies.append(send_g(22 + k, mine, mine, there))
    for copy in pending:
        copy.wait_send()
    for copy in copies:
        copy.wait_recv()
    gram[...] = (full_g[...] + other_g[...]) * (1.0 / (PER * 2 * RING * RING * DEPTH))

    for copy in copies:
        copy.wait_send()


def cholesky_kernel(gram, sketch_in, factor, sketch, work, upper, rows, sems):
    fetch = pltpu.make_async_copy(sketch_in, rows, sems.at[0])
    fetch.start()
    work[...] = gram[...]
    row = lax.broadcasted_iota(jnp.int32, (PANEL, COLS), 0)
    lane = lax.broadcasted_iota(jnp.int32, (PANEL, COLS), 1)
    fetch.wait()
    store = pltpu.make_async_copy(rows, sketch, sems.at[1])
    store.start()
    for base in range(0, COLS, PANEL):
        panel = work[pl.ds(base, PANEL), :]
        columns = [jnp.broadcast_to(panel[:, base + k : base + k + 1], (PANEL, COLS)) for k in range(PANEL)]
        pivots = jnp.ones((PANEL, COLS), F32)
        for j in range(PANEL):
            pivot = columns[j][j : j + 1, :]
            pivots = jnp.where(row == j, columns[j], pivots)
            factors = jnp.where(row > j, columns[j] * (1.0 / pivot), 0.0)
            for k in range(j + 1, PANEL):
                columns[k] = columns[k] - factors * columns[k][j : j + 1, :]
            panel = panel - factors * panel[j : j + 1, :]
        root = lax.rsqrt(pivots)
        root = root * (1.5 - 0.5 * pivots * root * root)
        scaled = jnp.where(lane >= base + row, panel * root, 0.0)
        upper[pl.ds(base, PANEL), :] = scaled
        if base + PANEL < COLS:
            update = exact_product(scaled)
            after = base + PANEL
            work[pl.ds(after, COLS - after), :] -= update[after:, :]
    factor[...] = upper[...].T
    store.wait()


def shards(matrix, flips, picks):
    vmem = pl.BlockSpec(memory_space=pltpu.VMEM)
    half_a = (DEPTH, 2, RING // 2 * PER, COLS)
    dma = pltpu.SemaphoreType.DMA
    sketch, gram = pl.pallas_call(
        kernel,
        name="blendenpik",
        out_shape=(
            jax.ShapeDtypeStruct((PER, COLS), F32),
            jax.ShapeDtypeStruct((COLS, COLS), F32),
        ),
        in_specs=[pl.BlockSpec(memory_space=pltpu.HBM)] * 3,
        out_specs=(vmem, vmem),
        scratch_shapes=[
            pltpu.VMEM((ROWS, COLS), F32),
            pltpu.VMEM((ROWS, COLS), F32),
            pltpu.VMEM((ROWS // COLS, COLS), jnp.int32),
            pltpu.VMEM((ROWS // COLS, COLS), jnp.int32),
            pltpu.VMEM((BLOCK, BLOCK), BF16),
            pltpu.VMEM((ROWS, COLS), F32),
            pltpu.VMEM((RING * RING * DEPTH, 1, PER), jnp.int32),
            pltpu.SMEM((RING * RING * DEPTH, 1, PER), jnp.int32),
            pltpu.VMEM((DEPTH, 8, RING // 2 * PER, COLS), F32),
            pltpu.VMEM(half_a, F32),
            pltpu.VMEM(half_a, F32),
            pltpu.VMEM(half_a, F32),
            pltpu.VMEM((DEPTH, RING, PER, COLS), F32),
            pltpu.VMEM((DEPTH, RING, PER, COLS), F32),
            pltpu.VMEM((RING, PER, COLS), F32),
            pltpu.VMEM((RING - 1, PER, COLS), F32),
            pltpu.VMEM((COLS, COLS), F32),
            pltpu.VMEM((RING * RING, PIECE, COLS), F32),
            pltpu.VMEM((DEPTH, PIECE, COLS), F32),
            pltpu.VMEM((COLS, COLS), F32),
            pltpu.VMEM((COLS, COLS), F32),
            dma((CHUNKS,)),
            dma((1,)),
            pltpu.SemaphoreType.REGULAR((3,)),
            pltpu.SemaphoreType.REGULAR,
            dma((CHUNKS,)),
            dma((CHUNKS,)),
            dma((2,)),
            dma((14,)),
            dma((14,)),
            dma((1,)),
            dma((DEPTH,)),
            dma((DEPTH, 6)),
            dma((DEPTH, 6)),
            dma((3,)),
            dma((3,)),
            dma((DEPTH,)),
            dma((DEPTH,)),
            dma((54,)),
            dma((54,)),
        ],
        compiler_params=pltpu.CompilerParams(
            collective_id=0, has_side_effects=True, vmem_limit_bytes=67043328
        ),
    )(matrix, flips.reshape(ROWS // COLS, COLS), picks.reshape(1, PER))
    hbm = pl.BlockSpec(memory_space=pltpu.HBM)
    factor, sketch = pl.pallas_call(
        cholesky_kernel,
        name="factor",
        out_shape=(jax.ShapeDtypeStruct((COLS, COLS), F32), jax.ShapeDtypeStruct((PER, COLS), F32)),
        in_specs=[vmem, hbm],
        out_specs=(vmem, hbm),
        scratch_shapes=[
            pltpu.VMEM((COLS, COLS), F32),
            pltpu.VMEM((COLS, COLS), F32),
            pltpu.VMEM((PER, COLS), F32),
            dma((2,)),
        ],
    )(gram, sketch)
    return (sketch, factor)


def solution(mesh):
    placed = (P("rows", None), P("rows"), P("rows"))
    return jax.shard_map(
        shards, mesh=mesh, in_specs=placed, out_specs=(P("rows", None), P()), check_vma=False
    )
```
